512 devices in a mesh: leaf: 32 (over x, y, core), row: 16 (over z).
Axes of the slice: x: 4, y: 4, z: 16, core: 2. Of those that a mesh axis runs over, the one named last changes fastest.
Arguments:
- rhs: bfloat16 [32, 16, 189, 512], P('leaf', 'row'), may hold values from -6 to 6
- inv_diag: bfloat16 [32, 16, 189, 1536], P('leaf', 'row'), may hold values from -0.15625 to 0.15625
- off_diag: bfloat16 [32, 16, 96, 12384], P('leaf', 'row'), may hold values from -0.0390625 to 0.0390625
- pair_mask: int32 [32, 16, 15], P('leaf', 'row'), may hold values 0 or 1
Outputs:
- solution: float32 [32, 16, 189, 512], P('leaf', 'row')
The draws below stay inside these ranges and needn't reach their ends.
All inputs are finite; a program needn't handle non-finite values. No bound on the sum of `pair_mask` on one device may be relied on, other than what follows from the above.
Results may differ from the reference program's by a relative error of at most 0.0065.
Values may be sent and summed in bfloat16 or wider, within the bound.
No kernel may reach another device: no remote copies, remote signals or barrier semaphores. Data moves between devices by JAX's collectives and lax.ppermute only.
A program may use at most 64 MiB of HBM per device.

```python
import jax
import jax.numpy as jnp

W = 1536
R = 512
LEVELS = 5
PACK = 189
QCOLS = 12384
PAIRS = 15
N_LEAF = 32
N_ROW = 16


def with_ends(drawn, own_key, smallest, high):
    longest = drawn.shape.index(max(drawn.shape))
    spots = []
    for shift in (0, 1):
        where = [jax.random.randint(jax.random.fold_in(own_key, axis), (), 0, length) for axis, length in enumerate(drawn.shape)]
        where[longest] = (where[longest] + shift) % drawn.shape[longest]
        spots.append(tuple(where))
    return drawn.at[spots[0]].set(smallest).at[spots[1]].set(high)


def levels(rng, shape, pieces, smallest, largest):
    factor_of = 1.0
    for dim, blocks in pieces:
        draws = jax.random.uniform(jax.random.fold_in(jax.random.fold_in(rng, 6), dim), (blocks,), jnp.float32, smallest / len(pieces), largest / len(pieces))
        factor_of = factor_of * jnp.repeat(jnp.exp(draws), shape[dim] // blocks).reshape((-1,) + (1,) * (len(shape) - 1 - dim))
    return factor_of


def noise(rng, shape, scale, bound, cuts=(), dtype=jnp.bfloat16):
    values = scale * jax.random.normal(rng, shape, jnp.float32)
    if cuts:
        values = values * levels(rng, shape, cuts, -0.22, 0.18)
    return jnp.clip(values, -bound, bound).astype(dtype)


def setup_inputs(seed: int = 0) -> dict:
    splits = jax.random.split(jax.random.key(seed), 5)
    rhs = noise(splits[0], (N_LEAF, N_ROW, PACK, R), 1.0, 6.0, ((0, 32), (1, 16)))
    inv_diag = noise(splits[1], (N_LEAF, N_ROW, PACK, W), W ** -0.5, 0.15625, ((0, 32), (1, 16)))
    off_diag = noise(splits[2], (N_LEAF, N_ROW, W // N_ROW, QCOLS), (W * N_LEAF // 2) ** -0.5, 0.0390625, ((0, 32), (1, 16)))
    pair_mask = with_ends((jax.random.randint(splits[3], (N_LEAF, N_ROW, PAIRS), 0, 4) < 3).astype(jnp.int32), jax.random.fold_in(splits[3], 1), 0, 1)
    return dict(rhs=rhs, inv_diag=inv_diag, off_diag=off_diag, pair_mask=pair_mask)


def split_level(packed, height_lv):
    height = W // (2 ** height_lv * N_ROW)
    offset = 0
    for below in range(height_lv):
        offset += W // (2 ** below * N_ROW)
    sliced = packed[:, :, offset:offset + height, :]
    node_count = N_LEAF // 2 ** height_lv
    return sliced.reshape(node_count, W, sliced.shape[-1])


def join_level(nodes_arr, height_lv):
    height = W // (2 ** height_lv * N_ROW)
    return nodes_arr.reshape(N_LEAF, N_ROW, height, nodes_arr.shape[-1])


def column_start(ancestor, source):
    offset = 0
    for higher in range(1, ancestor):
        for within in range(higher):
            offset += W // 2 ** within
    for within in range(source):
        offset += W // 2 ** within
    return offset


def ancestor_update(off_diag, pair_mask, rounded, ancestor):
    strip_rows = W // N_ROW
    summed = jnp.zeros((N_LEAF, N_ROW, strip_rows, R), jnp.float32)
    for source in range(ancestor):
        span_cols = W // 2 ** source
        first_col = column_start(ancestor, source)
        panel_part = off_diag[:, :, :, first_col:first_col + span_cols].astype(jnp.float32)
        pair_live = pair_mask[:, :, ancestor * (ancestor - 1) // 2 + source].astype(jnp.float32)
        leaf_parts = rounded[source].reshape(N_LEAF, span_cols, R).astype(jnp.float32)
        product = jnp.einsum('gpqc,gcn->gpqn', panel_part, leaf_parts)
        summed = summed + product * pair_live[:, :, None, None]
    height = W // (2 ** ancestor * N_ROW)
    node_count = N_LEAF // 2 ** ancestor
    summed = summed.reshape(node_count, 2 ** ancestor, N_ROW, 2 ** ancestor, height, R).sum(axis=1)
    return jnp.transpose(summed, (0, 2, 1, 3, 4)).reshape(node_count, W, R)


def reference(rhs, inv_diag, off_diag, pair_mask):
    solutions = []
    rounded = []
    for ancestor in range(LEVELS + 1):
        right_side = split_level(rhs, ancestor).astype(jnp.float32)
        if ancestor > 0:
            right_side = right_side - ancestor_update(off_diag, pair_mask, rounded, ancestor)
        reduced = right_side.astype(jnp.bfloat16)
        inverse = split_level(inv_diag, ancestor).astype(jnp.float32)
        solved = jnp.einsum('jvw,jwn->jvn', inverse, reduced.astype(jnp.float32))
        rounded.append(solved.astype(jnp.bfloat16))
        solutions.append(join_level(solved, ancestor))
    return jnp.concatenate(solutions, axis=2)
```

```python
import jax
import jax.numpy as jnp
from jax import lax
from jax.sharding import PartitionSpec as P

F32 = jnp.float32
BF16 = jnp.bfloat16


def column_start(ancestor, source, width_all):
    offset = 0
    for higher in range(1, ancestor):
        for within in range(higher):
            offset += width_all // 2**within
    for within in range(source):
        offset += width_all // 2**within
    return offset


def dot(a, b):
    return jnp.dot(a, b, preferred_element_type=F32)


def dot_t(a, b):
    return lax.dot_general(a, b, (((1,), (b.ndim - 1,)), ((), ())), preferred_element_type=F32)


def core_swap(block):
    count = lax.axis_size("leaf")
    return lax.ppermute(block, "leaf", [(i, i ^ 1) for i in range(count)])


def leaf_groups(size):
    count = lax.axis_size("leaf")
    return [[first + i for i in range(size)] for first in range(0, count, size)]


def leaf_scatter(pieces):
    size = pieces.shape[0]
    return lax.all_to_all(pieces, "leaf", 0, 0, tiled=True, axis_index_groups=leaf_groups(size))


def leaf_everyone(block, size):
    return leaf_scatter(jnp.broadcast_to(block, (size, *block.shape)))


def shards(rhs, inv_diag, off_diag, pair_mask):
    rows_n = lax.axis_size("row")
    leaves = lax.axis_size("leaf")
    levels = leaves.bit_length() - 1
    width = inv_diag.shape[3]
    cols = rhs.shape[3]
    strip = width // rows_n
    half = cols // 2
    sub = half // rows_n
    leaf = lax.axis_index("leaf")
    core = leaf % 2
    first_core = core == 0
    b_all = rhs[0, 0]
    d_all = inv_diag[0, 0]
    panels = off_diag[0, 0]
    live = pair_mask[0, 0]
    heights = [strip >> m for m in range(levels + 1)]
    starts = [sum(heights[:m]) for m in range(levels + 1)]

    def panel(m, l):
        first = column_start(m, l, width)
        return panels[:, first : first + (width >> l)]

    def alive(m, l, dtype):
        return live[m * (m - 1) // 2 + l].astype(dtype)

    def masked(m, l):
        return panel(m, l) * alive(m, l, BF16)

    d_own0 = d_all[: heights[0]]
    d_full0 = lax.all_gather(d_own0, "row", axis=0, tiled=True)
    b0 = b_all[: heights[0]]
    z0 = jnp.concatenate(
        [
            lax.all_gather(b0[:, :half], "row", axis=0, tiled=True),
            lax.all_gather(b0[:, half:], "row", axis=0, tiled=True),
        ],
        axis=1,
    )

    d_own1 = d_all[starts[1] : starts[2]]
    mid = width // 2
    own1 = jnp.concatenate(
        [masked(m, 1) for m in range(2, levels + 1)] + [d_own1[:, :mid], d_own1[:, mid:]], axis=0
    )
    other1 = core_swap(own1)
    p_rows = strip * (levels - 1)
    p_own1 = own1[:p_rows]
    p_other1 = other1[:p_rows]
    d_other1 = jnp.concatenate(
        [other1[p_rows : p_rows + heights[1]], other1[p_rows + heights[1] :]], axis=1
    )

    upper_pairs = sorted(
        ((m, l) for l in range(2, levels) for m in range(l + 1, levels + 1)), key=lambda p: (p[1], p[0])
    )
    d_up = d_all[starts[2] :]
    d_rows = d_up.shape[0]
    d_pad = strip // 2
    d_up = jnp.concatenate([d_up, jnp.zeros((d_pad - d_rows, width), BF16)], axis=0)
    packed = jnp.concatenate(
        [jnp.concatenate([d_up[:, :mid], d_up[:, mid:]], axis=0)] + [masked(m, l) for m, l in upper_pairs], axis=1
    )
    packed, d_full0 = lax.optimization_barrier((packed, d_full0))
    everyone = lax.all_gather(packed, "row", axis=0, tiled=False)

    yb0 = dot(d_full0, z0).astype(BF16)
    out0 = dot(d_own0, z0)
    parts = []
    for m in range(1, levels + 1):
        placed = lax.dynamic_update_slice(
            jnp.zeros((strip, cols), BF16),
            b_all[starts[m] : starts[m] + heights[m]],
            (leaf % 2**m * heights[m], 0),
        )
        parts.append(placed.astype(F32) - dot(panel(m, 0), yb0) * alive(m, 0, F32))
    part = jnp.concatenate(parts, axis=0)
    kept = jnp.where(first_core, part[:, :half], part[:, half:])
    sent = jnp.where(first_core, part[:, half:], part[:, :half]).astype(BF16)
    part = kept + core_swap(sent).astype(F32)

    def natural1(block):
        pieces = lax.all_gather(block, "row", axis=0, tiled=False)
        return pieces.reshape(rows_n, 2, heights[1], half).transpose(1, 0, 2, 3).reshape(2, mid, half)

    z1 = natural1(part[:strip].astype(BF16)).reshape(width, half)
    y_own1 = dot(d_own1, z1)
    y_other1 = dot(d_other1, z1)
    yb1 = jnp.where(
        first_core,
        jnp.concatenate([y_own1, y_other1], axis=0),
        jnp.concatenate([y_other1, y_own1], axis=0),
    ).astype(BF16)
    y_got1 = core_swap(y_other1)
    out1 = jnp.where(
        first_core,
        jnp.concatenate([y_own1, y_got1], axis=1),
        jnp.concatenate([y_got1, y_own1], axis=1),
    )
    yn1 = natural1(yb1)
    here = jnp.where(first_core, yn1[0], yn1[1])
    there = jnp.where(first_core, yn1[1], yn1[0])
    part = part[strip:] - (dot(p_own1, here) + dot(p_other1, there))

    turned = part.T.astype(BF16).reshape(rows_n, sub, p_rows)
    turned = lax.all_to_all(turned, "row", 0, 0, tiled=True)

    def turned_of(m):
        return turned[:, :, (m - 2) * strip : (m - 1) * strip]

    def d_leaf(m):
        low = starts[m] - starts[2]
        left = everyone[:, low : low + heights[m], :mid]
        right = everyone[:, d_pad + low : d_pad + low + heights[m], :mid]
        return jnp.concatenate([left, right], axis=2).reshape(rows_n * heights[m], width)

    p_leaf = {}
    at = mid
    for m, l in upper_pairs:
        p_leaf[m, l] = everyone[:, :, at : at + (width >> l)]
        at += width >> l

    def natural(z, m):
        z = z.reshape(rows_n, 2 * sub, 2**m, heights[m])
        return z.transpose(1, 2, 0, 3).reshape(2 * sub, width)

    solved = []
    sums = {}
    for m in range(2, levels + 1):
        if m == 2:
            pieces = leaf_everyone(turned_of(2), 4).astype(F32)
            pieces = pieces.reshape(2, 2, rows_n, sub, strip).sum(axis=0).astype(BF16)
            z = pieces.transpose(1, 0, 2, 3).reshape(rows_n, 2 * sub, strip)
        else:
            size = 2**m
            mine = jnp.where(
                (jnp.arange(2) == core)[None, :, None, None], turned_of(m)[:, None], jnp.zeros((), BF16)
            ).reshape(rows_n, 2 * sub, strip)
            v = (mine.astype(F32) - sums[m]).astype(BF16)
            if size <= rows_n:
                v = v.reshape(size, rows_n // size, 2 * sub, strip)
                z = leaf_scatter(v).astype(F32).sum(axis=0).astype(BF16)
                z = leaf_everyone(z, size).reshape(rows_n, 2 * sub, strip)
            else:
                cut = size // rows_n
                v = v.reshape(rows_n, 2 * sub, cut, strip // cut).transpose(0, 2, 1, 3)
                v = v.reshape(size, 2 * sub, strip // cut)
                z = leaf_scatter(v).astype(F32).sum(axis=0).astype(BF16)
                z = leaf_everyone(z, size).reshape(rows_n, cut, 2 * sub, strip // cut)
                z = z.transpose(0, 2, 1, 3).reshape(rows_n, 2 * sub, strip)
        y = dot_t(natural(z, m), d_leaf(m))
        yb = y.astype(BF16)
        solved.append(yb.reshape(2 * sub, rows_n, heights[m]))
        for higher in range(m + 1, levels + 1):
            term = dot_t(yb, p_leaf[higher, m]).transpose(1, 0, 2)
            sums[higher] = term if m == 2 else sums[higher] + term

    done = jnp.concatenate(solved, axis=2).transpose(1, 0, 2)
    done = lax.all_to_all(done, "row", 0, 0, tiled=True)
    done = done.reshape(rows_n, 2, sub, d_rows).transpose(3, 1, 0, 2).reshape(d_rows, cols)
    return jnp.concatenate([out0, out1, done.astype(F32)], axis=0)[None, None]


def solution(mesh):
    in_specs = (
        P("leaf", "row", None, None),
        P("leaf", "row", None, None),
        P("leaf", "row", None, None),
        P("leaf", "row", None),
    )
    out_specs = P("leaf", "row", None, None)
    return jax.shard_map(shards, mesh=mesh, in_specs=in_specs, out_specs=out_specs, check_vma=False)
```

```python
import jax
import jax.numpy as jnp
from jax import lax
from jax.sharding import PartitionSpec as P

F32 = jnp.float32
BF16 = jnp.bfloat16


def column_start(ancestor, source, width_all):
    offset = 0
    for higher in range(1, ancestor):
        for within in range(higher):
            offset += width_all // 2**within
    for within in range(source):
        offset += width_all // 2**within
    return offset


def dot(a, b):
    return jnp.dot(a, b, preferred_element_type=F32)


def dot_t(a, b):
    return lax.dot_general(a, b, (((1,), (b.ndim - 1,)), ((), ())), preferred_element_type=F32)


def core_swap(block):
    count = lax.axis_size("leaf")
    return lax.ppermute(block, "leaf", [(i, i ^ 1) for i in range(count)])


def leaf_groups(size):
    count = lax.axis_size("leaf")
    return [[first + i for i in range(size)] for first in range(0, count, size)]


def leaf_scatter(pieces):
    size = pieces.shape[0]
    return lax.all_to_all(pieces, "leaf", 0, 0, tiled=True, axis_index_groups=leaf_groups(size))


def leaf_everyone(block, size):
    return leaf_scatter(jnp.broadcast_to(block, (size, *block.shape)))


def shards(rhs, inv_diag, off_diag, pair_mask):
    rows_n = lax.axis_size("row")
    leaves = lax.axis_size("leaf")
    levels = leaves.bit_length() - 1
    width = inv_diag.shape[3]
    cols = rhs.shape[3]
    strip = width // rows_n
    half = cols // 2
    sub = half // rows_n
    leaf = lax.axis_index("leaf")
    core = leaf % 2
    first_core = core == 0
    b_all = rhs[0, 0]
    d_all = inv_diag[0, 0]
    panels = off_diag[0, 0]
    live = pair_mask[0, 0]
    heights = [strip >> m for m in range(levels + 1)]
    starts = [sum(heights[:m]) for m in range(levels + 1)]

    def panel(m, l):
        first = column_start(m, l, width)
        return panels[:, first : first + (width >> l)]

    def alive(m, l, dtype):
        return live[m * (m - 1) // 2 + l].astype(dtype)

    def masked(m, l):
        return panel(m, l) * alive(m, l, BF16)

    d_own0 = d_all[: heights[0]]
    d_full0 = lax.all_gather(d_own0, "row", axis=0, tiled=True)
    b0 = b_all[: heights[0]]
    z0_left = lax.all_gather(b0[:, :half], "row", axis=0, tiled=True)
    z0_right = lax.all_gather(b0[:, half:], "row", axis=0, tiled=True)

    mid = width // 2
    upper_pairs = sorted(
        ((m, l) for l in range(2, levels) for m in range(l + 1, levels + 1)), key=lambda p: (p[1], p[0])
    )
    d_up = d_all[starts[2] :]
    d_rows = d_up.shape[0]
    d_pad = strip // 2
    d_up = jnp.concatenate([d_up, jnp.zeros((d_pad - d_rows, width), BF16)], axis=0)
    packed = jnp.concatenate(
        [jnp.concatenate([d_up[:, :mid], d_up[:, mid:]], axis=0)] + [masked(m, l) for m, l in upper_pairs], axis=1
    )
    packed, z0_left = lax.optimization_barrier((packed, z0_left))
    everyone = lax.all_gather(packed, "row", axis=0, tiled=False)

    z0 = jnp.concatenate([z0_left, z0_right], axis=1)
    yb0 = dot(d_full0, z0).astype(BF16)
    out0 = dot(d_own0, z0)
    parts = []
    for m in range(1, levels + 1):
        placed = lax.dynamic_update_slice(
            jnp.zeros((strip, cols), BF16),
            b_all[starts[m] : starts[m] + heights[m]],
            (leaf % 2**m * heights[m], 0),
        )
        parts.append(placed.astype(F32) - dot(panel(m, 0), yb0) * alive(m, 0, F32))
    def core_sum(part):
        kept = jnp.where(first_core, part[:, :half], part[:, half:])
        sent = jnp.where(first_core, part[:, half:], part[:, :half]).astype(BF16)
        return kept + core_swap(sent).astype(F32)

    d_own1 = d_all[starts[1] : starts[2]]
    z1 = core_sum(parts[0]).astype(BF16)
    z1 = lax.all_gather(z1, "row", axis=0, tiled=False)
    z1 = z1.reshape(rows_n, 2, heights[1], half).transpose(1, 0, 2, 3).reshape(width, half)
    z1_got = core_swap(z1)
    y_kept1 = dot(d_own1, z1)
    y_got1 = dot(d_own1, z1_got)
    out1 = jnp.where(
        first_core,
        jnp.concatenate([y_kept1, y_got1], axis=1),
        jnp.concatenate([y_got1, y_kept1], axis=1),
    )
    yb1 = lax.all_gather(out1.astype(BF16), "row", axis=0, tiled=True)
    parts = [
        parts[m - 1] - dot(panel(m, 1), yb1) * alive(m, 1, F32) for m in range(2, levels + 1)
    ]
    part = core_sum(jnp.concatenate(parts, axis=0))
    p_rows = strip * (levels - 1)

    turned = part.T.astype(BF16).reshape(rows_n, sub, p_rows)
    turned = lax.all_to_all(turned, "row", 0, 0, tiled=True)

    def turned_of(m):
        return turned[:, :, (m - 2) * strip : (m - 1) * strip]

    def d_leaf(m):
        low = starts[m] - starts[2]
        left = everyone[:, low : low + heights[m], :mid]
        right = everyone[:, d_pad + low : d_pad + low + heights[m], :mid]
        return jnp.concatenate([left, right], axis=2).reshape(rows_n * heights[m], width)

    p_leaf = {}
    at = mid
    for m, l in upper_pairs:
        p_leaf[m, l] = everyone[:, :, at : at + (width >> l)]
        at += width >> l

    def natural(z, m):
        z = z.reshape(rows_n, 2 * sub, 2**m, heights[m])
        return z.transpose(1, 2, 0, 3).reshape(2 * sub, width)

    solved = []
    sums = {}
    for m in range(2, levels + 1):
        if m == 2:
            pieces = leaf_everyone(turned_of(2), 4).astype(F32)
            pieces = pieces.reshape(2, 2, rows_n, sub, strip).sum(axis=0).astype(BF16)
            z = pieces.transpose(1, 0, 2, 3).reshape(rows_n, 2 * sub, strip)
        else:
            size = 2**m
            mine = jnp.where(
                (jnp.arange(2) == core)[None, :, None, None], turned_of(m)[:, None], jnp.zeros((), BF16)
            ).reshape(rows_n, 2 * sub, strip)
            v = (mine.astype(F32) - sums[m]).astype(BF16)
            if size <= rows_n:
                v = v.reshape(size, rows_n // size, 2 * sub, strip)
                z = leaf_scatter(v).astype(F32).sum(axis=0).astype(BF16)
                z = leaf_everyone(z, size).reshape(rows_n, 2 * sub, strip)
            else:
                cut = size // rows_n
                v = v.reshape(rows_n, 2 * sub, cut, strip // cut).transpose(0, 2, 1, 3)
                v = v.reshape(size, 2 * sub, strip // cut)
                z = leaf_scatter(v).astype(F32).sum(axis=0).astype(BF16)
                z = leaf_everyone(z, size).reshape(rows_n, cut, 2 * sub, strip // cut)
                z = z.transpose(0, 2, 1, 3).reshape(rows_n, 2 * sub, strip)
        y = dot_t(natural(z, m), d_leaf(m))
        yb = y.astype(BF16)
        solved.append(yb.reshape(2 * sub, rows_n, heights[m]))
        for higher in range(m + 1, levels + 1):
            term = dot_t(yb, p_leaf[higher, m]).transpose(1, 0, 2)
            sums[higher] = term if m == 2 else sums[higher] + term

    done = jnp.concatenate(solved, axis=2).transpose(1, 0, 2)
    done = lax.all_to_all(done, "row", 0, 0, tiled=True)
    done = done.reshape(rows_n, 2, sub, d_rows).transpose(3, 1, 0, 2).reshape(d_rows, cols)
    return jnp.concatenate([out0, out1, done.astype(F32)], axis=0)[None, None]


def solution(mesh):
    in_specs = (
        P("leaf", "row", None, None),
        P("leaf", "row", None, None),
        P("leaf", "row", None, None),
        P("leaf", "row", None),
    )
    out_specs = P("leaf", "row", None, None)
    return jax.shard_map(shards, mesh=mesh, in_specs=in_specs, out_specs=out_specs, check_vma=False)
```

```python
import jax
import jax.numpy as jnp
import numpy as np
from jax import lax
from jax.sharding import PartitionSpec as P

F32 = jnp.float32
BF16 = jnp.bfloat16


def column_start(ancestor, source, width_all):
    offset = 0
    for higher in range(1, ancestor):
        for within in range(higher):
            offset += width_all // 2**within
    for within in range(source):
        offset += width_all // 2**within
    return offset


def dot(a, b):
    return jnp.dot(a, b, preferred_element_type=F32)


def dot_t(a, b):
    return lax.dot_general(a, b, (((1,), (b.ndim - 1,)), ((), ())), preferred_element_type=F32)


def core_swap(block):
    count = lax.axis_size("leaf")
    return lax.ppermute(block, "leaf", [(i, i ^ 1) for i in range(count)])


def leaf_groups(size):
    count = lax.axis_size("leaf")
    return [[first + i for i in range(size)] for first in range(0, count, size)]


def leaf_scatter(pieces):
    size = pieces.shape[0]
    return lax.all_to_all(pieces, "leaf", 0, 0, tiled=True, axis_index_groups=leaf_groups(size))


def leaf_everyone(block, size):
    return leaf_scatter(jnp.broadcast_to(block, (size, *block.shape)))


def shards(rhs, inv_diag, off_diag, pair_mask):
    rows_n = lax.axis_size("row")
    leaves = lax.axis_size("leaf")
    levels = leaves.bit_length() - 1
    width = inv_diag.shape[3]
    cols = rhs.shape[3]
    strip = width // rows_n
    half = cols // 2
    sub = half // rows_n
    leaf = lax.axis_index("leaf")
    core = leaf & 1
    first_core = core == 0
    b_all = rhs[0, 0]
    d_all = inv_diag[0, 0]
    panels = off_diag[0, 0]
    live = pair_mask[0, 0]
    heights = [strip >> m for m in range(levels + 1)]
    starts = [sum(heights[:m]) for m in range(levels + 1)]

    def panel(m, l):
        first = column_start(m, l, width)
        return panels[:, first : first + (width >> l)]

    def alive(m, l, dtype):
        return live[m * (m - 1) // 2 + l].astype(dtype)

    def by_core(one, two):
        return jnp.where(first_core, one, two)

    d_own0 = d_all[: heights[0]]
    d_full0 = lax.all_gather(d_own0, "row", axis=0, tiled=True)
    b0 = b_all[: heights[0]]
    z0_left = lax.all_gather(b0[:, :half], "row", axis=0, tiled=True)
    z0_right = lax.all_gather(b0[:, half:], "row", axis=0, tiled=True)

    upper_pairs = sorted(
        ((m, l) for l in range(2, levels) for m in range(l + 1, levels + 1)), key=lambda p: (p[1], p[0])
    )
    p_cols = sum(width >> l for _, l in upper_pairs)
    pieces = [
        jnp.concatenate([panel(m, l) * alive(m, l, BF16) for m, l in upper_pairs], axis=1)
    ]
    d_first = {}
    at = strip
    for m in range(2, levels + 1):
        d_first[m] = at
        room = -heights[m] % 8
        rows = d_all[starts[m] : starts[m] + heights[m]]
        pieces.append(jnp.pad(rows, ((0, room), (0, p_cols - width))))
        at += heights[m] + room
    packed = jnp.concatenate(pieces, axis=0)
    packed, z0_left = lax.optimization_barrier((packed, z0_left))
    everyone = lax.all_gather(packed, "row", axis=0, tiled=False)

    tall = strip * levels
    base = np.concatenate([strip * (m - 1) + np.arange(heights[m]) for m in range(1, levels + 1)])
    bits = np.concatenate([np.full(heights[m], 2**m - 1) for m in range(1, levels + 1)])
    step = np.concatenate([np.full(heights[m], heights[m]) for m in range(1, levels + 1)])
    place = jnp.asarray(base, jnp.int32) + (leaf & jnp.asarray(bits, jnp.int32)) * jnp.asarray(step, jnp.int32)
    spread = (lax.broadcasted_iota(jnp.int32, (tall, base.size), 0) == place[None]).astype(BF16)
    b_up = b_all[strip:]
    b_up = by_core(b_up, jnp.concatenate([b_up[:, half:], b_up[:, :half]], axis=1))
    placed = dot(spread, b_up)

    z0_sent = by_core(z0_right, z0_left)
    z0_kept = by_core(z0_left, z0_right)
    live1 = alive(1, 0, F32)
    yb_sent = dot(d_full0, z0_sent).astype(BF16)
    sent = placed[:strip, half:] - dot(panel(1, 0), yb_sent) * live1
    got = core_swap(sent.astype(BF16))
    yb_kept = dot(d_full0, z0_kept).astype(BF16)
    kept = placed[:strip, :half] - dot(panel(1, 0), yb_kept) * live1
    yb0 = jnp.concatenate([yb_kept, yb_sent], axis=1)
    parts = [
        placed[strip * (m - 1) : strip * m] - dot(panel(m, 0), yb0) * alive(m, 0, F32)
        for m in range(2, levels + 1)
    ]

    d_own1 = d_all[starts[1] : starts[2]]
    z1 = (kept + got.astype(F32)).astype(BF16)
    z1 = lax.all_gather(z1, "row", axis=0, tiled=False)
    z1 = z1.reshape(rows_n, 2, heights[1], half).transpose(1, 0, 2, 3).reshape(width, half)
    z1_got = core_swap(z1)
    y_kept1 = dot(d_own1, z1)
    y_sent1 = dot(d_own1, z1_got)
    yb1 = jnp.concatenate([y_kept1, y_sent1], axis=1).astype(BF16)
    yb1, parts = lax.optimization_barrier((yb1, parts))
    yb1 = lax.all_gather(yb1, "row", axis=0, tiled=True)
    out0_kept = dot(d_own0, z0_kept)
    out0_sent = dot(d_own0, z0_sent)
    part = jnp.concatenate(
        [parts[m - 2] - dot(panel(m, 1), yb1) * alive(m, 1, F32) for m in range(2, levels + 1)], axis=0
    )
    part = part[:, :half] + core_swap(part[:, half:].astype(BF16)).astype(F32)
    p_rows = strip * (levels - 1)

    turned = part.T.astype(BF16).reshape(rows_n, sub, p_rows)
    turned = lax.all_to_all(turned, "row", 0, 0, tiled=True)

    def turned_of(m):
        return turned[:, :, (m - 2) * strip : (m - 1) * strip]

    def d_leaf(m):
        rows = everyone[:, d_first[m] : d_first[m] + heights[m], :width]
        return rows.reshape(rows_n * heights[m], width)

    p_leaf = {}
    at = 0
    for m, l in upper_pairs:
        p_leaf[m, l] = everyone[:, :strip, at : at + (width >> l)]
        at += width >> l

    def natural(z, m):
        z = z.reshape(rows_n, 2 * sub, 2**m, heights[m])
        return z.transpose(1, 2, 0, 3).reshape(2 * sub, width)

    solved = []
    sums = {}
    for m in range(2, levels + 1):
        if m == 2:
            pieces = leaf_everyone(turned_of(2), 4).astype(F32)
            pieces = pieces.reshape(2, 2, rows_n, sub, strip).sum(axis=0).astype(BF16)
            z = pieces.transpose(1, 0, 2, 3).reshape(rows_n, 2 * sub, strip)
        else:
            size = 2**m
            mine = jnp.where(
                (jnp.arange(2) == core)[None, :, None, None], turned_of(m)[:, None], jnp.zeros((), BF16)
            ).reshape(rows_n, 2 * sub, strip)
            v = (mine.astype(F32) - sums[m]).astype(BF16)
            v = v.reshape(size, rows_n * 2 * sub // size, strip)
            z = leaf_scatter(v).astype(F32).sum(axis=0).astype(BF16)
            z = leaf_everyone(z, size).reshape(rows_n, 2 * sub, strip)
        y = dot_t(natural(z, m), d_leaf(m))
        yb = y.astype(BF16)
        solved.append(yb.reshape(2 * sub, rows_n, heights[m]))
        for higher in range(m + 1, levels + 1):
            term = dot_t(yb, p_leaf[higher, m]).transpose(1, 0, 2)
            sums[higher] = term if m == 2 else sums[higher] + term

    d_rows = sum(heights[2:])
    done = jnp.concatenate(solved, axis=2).transpose(1, 0, 2)
    done = lax.all_to_all(done, "row", 0, 0, tiled=True)
    done = done.reshape(rows_n, 2, sub, d_rows).transpose(3, 1, 0, 2).reshape(d_rows, cols)
    head_kept = jnp.concatenate([out0_kept, y_kept1], axis=0)
    head_sent = jnp.concatenate([out0_sent, y_sent1], axis=0)
    head = by_core(
        jnp.concatenate([head_kept, head_sent], axis=1), jnp.concatenate([head_sent, head_kept], axis=1)
    )
    return jnp.concatenate([head, done.astype(F32)], axis=0)[None, None]


def solution(mesh):
    in_specs = (
        P("leaf", "row", None, None),
        P("leaf", "row", None, None),
        P("leaf", "row", None, None),
        P("leaf", "row", None),
    )
    out_specs = P("leaf", "row", None, None)
    return jax.shard_map(shards, mesh=mesh, in_specs=in_specs, out_specs=out_specs, check_vma=False)
```

```python
import jax
import jax.numpy as jnp
import numpy as np
from jax import lax
from jax.experimental import pallas as pl
from jax.experimental.pallas import tpu as pltpu
from jax.sharding import PartitionSpec as P

F32 = jnp.float32
BF16 = jnp.bfloat16


def column_start(ancestor, source, width_all):
    offset = 0
    for higher in range(1, ancestor):
        for within in range(higher):
            offset += width_all // 2**within
    for within in range(source):
        offset += width_all // 2**within
    return offset


def dot(a, b):
    return jnp.dot(a, b, preferred_element_type=F32)


def dot_t(a, b):
    return lax.dot_general(a, b, (((1,), (b.ndim - 1,)), ((), ())), preferred_element_type=F32)


def core_swap(block):
    count = lax.axis_size("leaf")
    return lax.ppermute(block, "leaf", [(i, i ^ 1) for i in range(count)])


def leaf_groups(size):
    count = lax.axis_size("leaf")
    return [[first + i for i in range(size)] for first in range(0, count, size)]


def leaf_scatter(pieces):
    size = pieces.shape[0]
    return lax.all_to_all(pieces, "leaf", 0, 0, tiled=True, axis_index_groups=leaf_groups(size))


def leaf_everyone(block, size):
    return leaf_scatter(jnp.broadcast_to(block, (size, *block.shape)))


def pack_upper(off_diag, inv_diag, live, pairs, d_start):
    strip, width = off_diag.shape[2], inv_diag.shape[3]
    d_rows = inv_diag.shape[2] - d_start
    first = min(column_start(m, l, width) for m, l in pairs) // 128 * 128
    span = off_diag.shape[3] - first
    total = sum(width >> l for _, l in pairs)

    def body(live_ref, off_ref, inv_ref, out_ref, p_ref, d_ref, sems):
        p_copy = pltpu.make_async_copy(off_ref.at[0, 0, :, pl.ds(first, span)], p_ref, sems.at[0])
        d_copy = pltpu.make_async_copy(inv_ref.at[0, 0, pl.ds(d_start, d_rows), :], d_ref, sems.at[1])
        p_copy.start()
        d_copy.start()
        d_copy.wait()
        out_ref[strip:, :] = jnp.zeros((out_ref.shape[0] - strip, total), BF16)
        out_ref[strip : strip + d_rows, :width] = d_ref[...]
        p_copy.wait()
        at = 0
        for m, l in pairs:
            low = column_start(m, l, width) - first
            wide = width >> l
            alive = live_ref[m * (m - 1) // 2 + l].astype(F32)
            block = p_ref[:, low : low + wide].astype(F32) * alive
            out_ref[:strip, at : at + wide] = block.astype(BF16)
            at += wide

    tall = (strip + d_rows + 15) // 16 * 16
    return pl.pallas_call(
        body,
        out_shape=jax.ShapeDtypeStruct((tall, total), BF16),
        in_specs=[
            pl.BlockSpec(memory_space=pltpu.SMEM),
            pl.BlockSpec(memory_space=pl.ANY),
            pl.BlockSpec(memory_space=pl.ANY),
        ],
        out_specs=pl.BlockSpec(memory_space=pltpu.VMEM),
        scratch_shapes=[
            pltpu.VMEM((strip, span), BF16),
            pltpu.VMEM((d_rows, width), BF16),
            pltpu.SemaphoreType.DMA((2,)),
        ],
        name="pack_upper",
    )(live, off_diag, inv_diag)


def shards(rhs, inv_diag, off_diag, pair_mask):
    rows_n = lax.axis_size("row")
    leaves = lax.axis_size("leaf")
    levels = leaves.bit_length() - 1
    width = inv_diag.shape[3]
    cols = rhs.shape[3]
    strip = width // rows_n
    half = cols // 2
    sub = half // rows_n
    leaf = lax.axis_index("leaf")
    core = leaf & 1
    first_core = core == 0
    b_all = rhs[0, 0]
    d_all = inv_diag[0, 0]
    panels = off_diag[0, 0]
    live = pair_mask[0, 0]
    heights = [strip >> m for m in range(levels + 1)]
    starts = [sum(heights[:m]) for m in range(levels + 1)]

    def panel(m, l):
        first = column_start(m, l, width)
        return panels[:, first : first + (width >> l)]

    def mask_rows(l):
        ancestors = range(l + 1, levels + 1)
        index = jnp.asarray(np.repeat([m * (m - 1) // 2 + l for m in ancestors], strip), jnp.int32)
        hit = index[:, None] == lax.broadcasted_iota(jnp.int32, (1, live.shape[0]), 1)
        return jnp.where(hit, live[None], 0).sum(axis=1, keepdims=True).astype(F32)

    def by_core(one, two):
        return jnp.where(first_core, one, two)

    d_own0 = d_all[: heights[0]]
    d_full0 = lax.all_gather(d_own0, "row", axis=0, tiled=True)
    b0 = b_all[: heights[0]]
    z0_left = lax.all_gather(b0[:, :half], "row", axis=0, tiled=True)
    z0_right = lax.all_gather(b0[:, half:], "row", axis=0, tiled=True)

    upper_pairs = sorted(
        ((m, l) for l in range(2, levels) for m in range(l + 1, levels + 1)), key=lambda p: (p[1], p[0])
    )
    d_first = {m: strip + starts[m] - starts[2] for m in range(2, levels + 1)}
    packed = pack_upper(off_diag, inv_diag, live, upper_pairs, starts[2])
    packed, z0_left = lax.optimization_barrier((packed, z0_left))
    everyone = lax.all_gather(packed, "row", axis=0, tiled=False)

    tall = strip * levels
    base = np.concatenate([strip * (m - 1) + np.arange(heights[m]) for m in range(1, levels + 1)])
    bits = np.concatenate([np.full(heights[m], 2**m - 1) for m in range(1, levels + 1)])
    step = np.concatenate([np.full(heights[m], heights[m]) for m in range(1, levels + 1)])
    place = jnp.asarray(base, jnp.int32) + (leaf & jnp.asarray(bits, jnp.int32)) * jnp.asarray(step, jnp.int32)
    spread = (lax.broadcasted_iota(jnp.int32, (tall, base.size), 0) == place[None]).astype(BF16)
    b_up = b_all[strip:]
    b_up = by_core(b_up, jnp.concatenate([b_up[:, half:], b_up[:, :half]], axis=1))
    placed = dot(spread, b_up)

    z0_sent = by_core(z0_right, z0_left)
    z0_kept = by_core(z0_left, z0_right)
    mask0, mask1 = lax.optimization_barrier((mask_rows(0), mask_rows(1)))
    live1 = mask0[:strip]
    yb_sent = dot(d_full0, z0_sent).astype(BF16)
    sent = placed[:strip, half:] - dot(panel(1, 0), yb_sent) * live1
    got = core_swap(sent.astype(BF16))
    yb_kept = dot(d_full0, z0_kept).astype(BF16)
    kept = placed[:strip, :half] - dot(panel(1, 0), yb_kept) * live1
    yb0 = jnp.concatenate([yb_kept, yb_sent], axis=1)
    parts = [
        placed[strip * (m - 1) : strip * m] - dot(panel(m, 0), yb0) * mask0[strip * (m - 1) : strip * m]
        for m in range(2, levels + 1)
    ]

    d_own1 = d_all[starts[1] : starts[2]]
    z1 = (kept + got.astype(F32)).astype(BF16)
    z1 = lax.all_gather(z1, "row", axis=0, tiled=False)
    z1 = z1.reshape(rows_n, 2, heights[1], half).transpose(1, 0, 2, 3).reshape(width, half)
    z1_got = core_swap(z1)
    y_kept1 = dot(d_own1, z1)
    y_sent1 = dot(d_own1, z1_got)
    yb1 = jnp.concatenate([y_kept1, y_sent1], axis=1).astype(BF16)
    yb1, parts = lax.optimization_barrier((yb1, parts))
    yb1 = lax.all_gather(yb1, "row", axis=0, tiled=True)
    out0_kept = dot(d_own0, z0_kept)
    out0_sent = dot(d_own0, z0_sent)
    part = jnp.concatenate(
        [
            parts[m - 2] - dot(panel(m, 1), yb1) * mask1[strip * (m - 2) : strip * (m - 1)]
            for m in range(2, levels + 1)
        ],
        axis=0,
    )
    part = part[:, :half] + core_swap(part[:, half:].astype(BF16)).astype(F32)
    p_rows = strip * (levels - 1)

    turned = part.T.astype(BF16).reshape(rows_n, sub, p_rows)
    turned = lax.all_to_all(turned, "row", 0, 0, tiled=True)

    def turned_of(m):
        return turned[:, :, (m - 2) * strip : (m - 1) * strip]

    def d_leaf(m):
        rows = everyone[:, d_first[m] : d_first[m] + heights[m], :width]
        return rows.reshape(rows_n * heights[m], width)

    p_leaf = {}
    at = 0
    for m, l in upper_pairs:
        p_leaf[m, l] = everyone[:, :strip, at : at + (width >> l)]
        at += width >> l

    def natural(z, m):
        z = z.reshape(rows_n, 2 * sub, 2**m, heights[m])
        return z.transpose(1, 2, 0, 3).reshape(2 * sub, width)

    solved = []
    sums = {}
    for m in range(2, levels + 1):
        if m == 2:
            pieces = leaf_everyone(turned_of(2), 4).astype(F32)
            pieces = pieces.reshape(2, 2, rows_n, sub, strip).sum(axis=0).astype(BF16)
            z = pieces.transpose(1, 0, 2, 3).reshape(rows_n, 2 * sub, strip)
        else:
            size = 2**m
            mine = jnp.where(
                (jnp.arange(2) == core)[None, :, None, None], turned_of(m)[:, None], jnp.zeros((), BF16)
            ).reshape(rows_n, 2 * sub, strip)
            v = (mine.astype(F32) - sums[m]).astype(BF16)
            v = v.reshape(size, rows_n * 2 * sub // size, strip)
            z = leaf_scatter(v).astype(F32).sum(axis=0).astype(BF16)
            z = leaf_everyone(z, size).reshape(rows_n, 2 * sub, strip)
        y = dot_t(natural(z, m), d_leaf(m))
        yb = y.astype(BF16)
        solved.append(yb.reshape(2 * sub, rows_n, heights[m]))
        for higher in range(m + 1, levels + 1):
            term = dot_t(yb, p_leaf[higher, m]).transpose(1, 0, 2)
            sums[higher] = term if m == 2 else sums[higher] + term

    d_rows = sum(heights[2:])
    done = jnp.concatenate(solved, axis=2).transpose(1, 0, 2)
    done = lax.all_to_all(done, "row", 0, 0, tiled=True)
    done = done.reshape(rows_n, 2, sub, d_rows).transpose(3, 1, 0, 2).reshape(d_rows, cols)
    head_kept = jnp.concatenate([out0_kept, y_kept1], axis=0)
    head_sent = jnp.concatenate([out0_sent, y_sent1], axis=0)
    head = by_core(
        jnp.concatenate([head_kept, head_sent], axis=1), jnp.concatenate([head_sent, head_kept], axis=1)
    )
    return jnp.concatenate([head, done.astype(F32)], axis=0)[None, None]


def solution(mesh):
    in_specs = (
        P("leaf", "row", None, None),
        P("leaf", "row", None, None),
        P("leaf", "row", None, None),
        P("leaf", "row", None),
    )
    out_specs = P("leaf", "row", None, None)
    return jax.shard_map(shards, mesh=mesh, in_specs=in_specs, out_specs=out_specs, check_vma=False)
```

```python
import jax
import jax.numpy as jnp
import numpy as np
from jax import lax
from jax.experimental import pallas as pl
from jax.experimental.pallas import tpu as pltpu
from jax.sharding import PartitionSpec as P

F32 = jnp.float32
BF16 = jnp.bfloat16


def column_start(ancestor, source, width_all):
    offset = 0
    for higher in range(1, ancestor):
        for within in range(higher):
            offset += width_all // 2**within
    for within in range(source):
        offset += width_all // 2**within
    return offset


def dot(a, b):
    return jnp.dot(a, b, preferred_element_type=F32)


def dot_t(a, b):
    return lax.dot_general(a, b, (((1,), (b.ndim - 1,)), ((), ())), preferred_element_type=F32)


def core_swap(block):
    count = lax.axis_size("leaf")
    return lax.ppermute(block, "leaf", [(i, i ^ 1) for i in range(count)])


def leaf_groups(size):
    count = lax.axis_size("leaf")
    return [[first + i for i in range(size)] for first in range(0, count, size)]


def leaf_scatter(pieces):
    size = pieces.shape[0]
    return lax.all_to_all(pieces, "leaf", 0, 0, tiled=True, axis_index_groups=leaf_groups(size))


def leaf_everyone(block, size):
    return leaf_scatter(jnp.broadcast_to(block, (size, *block.shape)))


def pack_upper(off_diag, inv_diag, live, pairs, d_start):
    strip, width = off_diag.shape[2], inv_diag.shape[3]
    mid = width // 2
    top = max(m for m, _ in pairs)
    d_rows = inv_diag.shape[2] - d_start
    d_top = strip >> top
    d_low = d_rows - d_top
    first = min(column_start(m, l, width) for m, l in pairs) // 128 * 128
    span = off_diag.shape[3] - first
    low_pairs = [p for p in pairs if p[0] < top]
    top_pairs = [p for p in pairs if p[0] == top]
    low_cols = mid + sum(width >> l for _, l in low_pairs)
    room = -2 * d_top % 8

    def body(live_ref, off_ref, inv_ref, low_ref, top_ref, p_ref, d_ref, sems):
        p_copy = pltpu.make_async_copy(off_ref.at[0, 0, :, pl.ds(first, span)], p_ref, sems.at[0])
        d_copy = pltpu.make_async_copy(inv_ref.at[0, 0, pl.ds(d_start, d_rows), :], d_ref, sems.at[1])
        p_copy.start()
        d_copy.start()
        d_copy.wait()
        rows = d_ref[...].astype(F32)
        pad = jnp.zeros((strip // 2 - d_low, mid), F32)
        low = [rows[:d_low, :mid], pad, rows[:d_low, mid:], pad]
        low_ref[:, :mid] = jnp.concatenate(low, axis=0).astype(BF16)
        under = [rows[d_low:, :mid], rows[d_low:, mid:], jnp.zeros((room, mid), F32)]
        top_ref[strip:, :] = jnp.concatenate(under, axis=0).astype(BF16)
        p_copy.wait()

        def put(ref, at, some):
            for m, l in some:
                start = column_start(m, l, width) - first
                wide = width >> l
                alive = live_ref[m * (m - 1) // 2 + l].astype(F32)
                block = p_ref[:, start : start + wide].astype(F32) * alive
                ref[:strip, at : at + wide] = block.astype(BF16)
                at += wide
            return at

        put(low_ref, mid, low_pairs)
        end = put(top_ref, 0, top_pairs)
        top_ref[:strip, end:] = jnp.zeros((strip, mid - end), BF16)

    return pl.pallas_call(
        body,
        out_shape=(
            jax.ShapeDtypeStruct((strip, low_cols), BF16),
            jax.ShapeDtypeStruct((strip + 2 * d_top + room, mid), BF16),
        ),
        in_specs=[
            pl.BlockSpec(memory_space=pltpu.SMEM),
            pl.BlockSpec(memory_space=pl.ANY),
            pl.BlockSpec(memory_space=pl.ANY),
        ],
        out_specs=(pl.BlockSpec(memory_space=pltpu.VMEM), pl.BlockSpec(memory_space=pltpu.VMEM)),
        scratch_shapes=[
            pltpu.VMEM((strip, span), BF16),
            pltpu.VMEM((d_rows, width), BF16),
            pltpu.SemaphoreType.DMA((2,)),
        ],
        name="pack_upper",
    )(live, off_diag, inv_diag)


def level_zero(core, live, inverse, z_left, z_right, off_diag, placed):
    rows_n, both, width = inverse.shape
    half = z_left.shape[1]
    strip = off_diag.shape[2]
    under = both - strip
    parts = 2
    tall = width // parts
    each = rows_n // parts

    def body(core_ref, live_ref, inv_ref, left_ref, right_ref, off_ref, placed_ref, *rest):
        y_ref, kept_ref, sent_ref, d1_ref, d_ref, zl_ref, zr_ref, p_ref, sems = rest

        def d_copy(r):
            dst = d_ref.at[pl.ds(strip * r, strip), :]
            return pltpu.make_async_copy(inv_ref.at[r, pl.ds(0, strip), :], dst, sems.at[r])

        def d1_copy(r):
            dst = d1_ref.at[pl.ds(under * r, under), :]
            return pltpu.make_async_copy(inv_ref.at[r, pl.ds(strip, under), :], dst, sems.at[rows_n + r])

        left = pltpu.make_async_copy(left_ref, zl_ref, sems.at[2 * rows_n])
        right = pltpu.make_async_copy(right_ref, zr_ref, sems.at[2 * rows_n + 1])
        panel = pltpu.make_async_copy(off_ref.at[0, 0, :, pl.ds(0, width)], p_ref, sems.at[2 * rows_n + 2])
        left.start()
        right.start()
        for r in range(rows_n):
            d_copy(r).start()
        panel.start()
        for r in range(rows_n):
            d1_copy(r).start()
        left.wait()
        right.wait()
        first_core = core_ref[0] == 0
        z_kept = jnp.where(first_core, zl_ref[...], zr_ref[...])
        z_sent = jnp.where(first_core, zr_ref[...], zl_ref[...])
        z = jnp.concatenate([z_kept, z_sent], axis=1)
        total = jnp.zeros((strip, 2 * half), F32)
        for i in range(parts):
            for r in range(each * i, each * (i + 1)):
                d_copy(r).wait()
            y = dot(d_ref[tall * i : tall * (i + 1), :], z).astype(BF16)
            y_ref[tall * i : tall * (i + 1), :] = y
            if i == 0:
                panel.wait()
            total = total + dot(p_ref[:, tall * i : tall * (i + 1)], y)
        v = placed_ref[...] - total * live_ref[0].astype(F32)
        kept_ref[...] = v[:, :half]
        sent_ref[...] = v[:, half:].astype(BF16)
        for r in range(rows_n):
            d1_copy(r).wait()

    vmem = pl.BlockSpec(memory_space=pltpu.VMEM)
    smem = pl.BlockSpec(memory_space=pltpu.SMEM)
    hbm = pl.BlockSpec(memory_space=pl.ANY)
    return pl.pallas_call(
        body,
        out_shape=(
            jax.ShapeDtypeStruct((width, 2 * half), BF16),
            jax.ShapeDtypeStruct((strip, half), F32),
            jax.ShapeDtypeStruct((strip, half), BF16),
            jax.ShapeDtypeStruct((rows_n * under, width), BF16),
        ),
        in_specs=[smem, smem, hbm, hbm, hbm, hbm, vmem],
        out_specs=(vmem, vmem, vmem, hbm),
        scratch_shapes=[
            pltpu.VMEM((width, width), BF16),
            pltpu.VMEM((width, half), BF16),
            pltpu.VMEM((width, half), BF16),
            pltpu.VMEM((strip, width), BF16),
            pltpu.SemaphoreType.DMA((2 * rows_n + 3,)),
        ],
        compiler_params=pltpu.CompilerParams(vmem_limit_bytes=40 << 20),
        name="level_zero",
    )(core, live, inverse, z_left, z_right, off_diag, placed)


def shards(rhs, inv_diag, off_diag, pair_mask):
    rows_n = lax.axis_size("row")
    leaves = lax.axis_size("leaf")
    levels = leaves.bit_length() - 1
    width = inv_diag.shape[3]
    cols = rhs.shape[3]
    strip = width // rows_n
    half = cols // 2
    sub = half // rows_n
    leaf = lax.axis_index("leaf")
    core = leaf & 1
    first_core = core == 0
    b_all = rhs[0, 0]
    d_all = inv_diag[0, 0]
    panels = off_diag[0, 0]
    live = pair_mask[0, 0]
    heights = [strip >> m for m in range(levels + 1)]
    starts = [sum(heights[:m]) for m in range(levels + 1)]

    def panel(m, l):
        first = column_start(m, l, width)
        return panels[:, first : first + (width >> l)]

    def mask_rows(l):
        ancestors = range(l + 1, levels + 1)
        index = jnp.asarray(np.repeat([m * (m - 1) // 2 + l for m in ancestors], strip), jnp.int32)
        hit = index[:, None] == lax.broadcasted_iota(jnp.int32, (1, live.shape[0]), 1)
        return jnp.where(hit, live[None], 0).sum(axis=1, keepdims=True).astype(F32)

    def by_core(one, two):
        return jnp.where(first_core, one, two)

    d_low = lax.all_gather(d_all[: starts[2]], "row", axis=0, tiled=False)
    b0 = b_all[: heights[0]]
    z0_left = lax.all_gather(b0[:, :half], "row", axis=0, tiled=True)
    z0_right = lax.all_gather(b0[:, half:], "row", axis=0, tiled=True)

    mid = width // 2
    upper_pairs = sorted(
        ((m, l) for l in range(2, levels) for m in range(l + 1, levels + 1)), key=lambda p: (p[1], p[0])
    )
    packed_low, packed_top = pack_upper(off_diag, inv_diag, live, upper_pairs, starts[2])
    packed_low, z0_left = lax.optimization_barrier((packed_low, z0_left))
    upper_low = lax.all_gather(packed_low, "row", axis=0, tiled=False)

    tall = strip * levels
    base = np.concatenate([strip * (m - 1) + np.arange(heights[m]) for m in range(1, levels + 1)])
    bits = np.concatenate([np.full(heights[m], 2**m - 1) for m in range(1, levels + 1)])
    step = np.concatenate([np.full(heights[m], heights[m]) for m in range(1, levels + 1)])
    place = jnp.asarray(base, jnp.int32) + (leaf & jnp.asarray(bits, jnp.int32)) * jnp.asarray(step, jnp.int32)
    spread = (lax.broadcasted_iota(jnp.int32, (tall, base.size), 0) == place[None]).astype(BF16)
    b_up = b_all[strip:]
    b_up = by_core(b_up, jnp.concatenate([b_up[:, half:], b_up[:, :half]], axis=1))
    placed = dot(spread, b_up)

    mask0, mask1 = lax.optimization_barrier((mask_rows(0), mask_rows(1)))
    yb0, kept, sent, d_leaf1 = level_zero(
        core.reshape(1), live, d_low, z0_left, z0_right, off_diag, placed[:strip]
    )
    got = core_swap(sent)
    packed_top, kept = lax.optimization_barrier((packed_top, kept))
    upper_top = lax.all_gather(packed_top, "row", axis=0, tiled=False)
    parts = [
        placed[strip * (m - 1) : strip * m] - dot(panel(m, 0), yb0) * mask0[strip * (m - 1) : strip * m]
        for m in range(2, levels + 1)
    ]

    z1 = (kept + got.astype(F32)).astype(BF16)
    z1 = lax.all_gather(z1, "row", axis=0, tiled=False)
    z1 = z1.reshape(rows_n, 2, heights[1], half).transpose(1, 0, 2, 3).reshape(width, half)
    z1_got = core_swap(z1)
    yb_kept1 = dot(d_leaf1, z1).astype(BF16)
    z1_got, yb_kept1, parts = lax.optimization_barrier((z1_got, yb_kept1, parts))
    yb1 = jnp.concatenate([yb_kept1, dot(d_leaf1, z1_got).astype(BF16)], axis=1)
    d_own0 = d_all[: heights[0]]
    d_own1 = d_all[starts[1] : starts[2]]
    y_kept1 = dot(d_own1, z1)
    y_sent1 = dot(d_own1, z1_got)
    out0_kept = dot(d_own0, by_core(z0_left, z0_right))
    out0_sent = dot(d_own0, by_core(z0_right, z0_left))
    part = jnp.concatenate(
        [
            parts[m - 2] - dot(panel(m, 1), yb1) * mask1[strip * (m - 2) : strip * (m - 1)]
            for m in range(2, levels + 1)
        ],
        axis=0,
    )
    part = part[:, :half] + core_swap(part[:, half:].astype(BF16)).astype(F32)
    p_rows = strip * (levels - 1)

    turned = part.T.astype(BF16).reshape(rows_n, sub, p_rows)
    turned = lax.all_to_all(turned, "row", 0, 0, tiled=True)

    def turned_of(m):
        return turned[:, :, (m - 2) * strip : (m - 1) * strip]

    def d_leaf(m, low, top):
        high = heights[m]
        if m < levels:
            at = starts[m] - starts[2]
            left = low[:, at : at + high, :mid]
            right = low[:, strip // 2 + at : strip // 2 + at + high, :mid]
        else:
            left = top[:, strip : strip + high]
            right = top[:, strip + high : strip + 2 * high]
        return jnp.concatenate([left, right], axis=2).reshape(rows_n * high, width)

    p_first = {}
    at = mid
    for m, l in upper_pairs:
        if m < levels:
            p_first[m, l] = at
            at += width >> l
    at = 0
    for m, l in upper_pairs:
        if m == levels:
            p_first[m, l] = at
            at += width >> l

    def p_leaf(m, l, low, top):
        block = low if m < levels else top
        return block[:, :strip, p_first[m, l] : p_first[m, l] + (width >> l)]

    def natural(z, m):
        z = z.reshape(rows_n, 2 * sub, 2**m, heights[m])
        return z.transpose(1, 2, 0, 3).reshape(2 * sub, width)

    solved = []
    terms = {m: [] for m in range(3, levels + 1)}
    for m in range(2, levels + 1):
        if m == 2:
            pieces = jnp.broadcast_to(turned_of(2), (4, rows_n, sub, strip))
            pieces, upper_low = lax.optimization_barrier((pieces, upper_low))
            pieces = leaf_scatter(pieces).astype(F32)
            pieces = pieces.reshape(2, 2, rows_n, sub, strip).sum(axis=0).astype(BF16)
            z = pieces.transpose(1, 0, 2, 3).reshape(rows_n, 2 * sub, strip)
        else:
            size = 2**m
            mine = jnp.where(
                (jnp.arange(2) == core)[None, :, None, None], turned_of(m)[:, None], jnp.zeros((), BF16)
            ).reshape(rows_n, 2 * sub, strip)
            v = mine.astype(F32)
            for l, yb in terms[m]:
                v = v - dot_t(yb, p_leaf(m, l, upper_low, upper_top)).transpose(1, 0, 2)
            v = v.astype(BF16).reshape(size, rows_n * 2 * sub // size, strip)
            z = leaf_scatter(v).astype(F32).sum(axis=0).astype(BF16)
            if m == levels - 1:
                z, upper_top = lax.optimization_barrier((z, upper_top))
            z = leaf_everyone(z, size).reshape(rows_n, 2 * sub, strip)
        y = dot_t(natural(z, m), d_leaf(m, upper_low, upper_top))
        yb = y.astype(BF16)
        solved.append(yb.reshape(2 * sub, rows_n, heights[m]))
        for higher in range(m + 1, levels + 1):
            terms[higher].append((m, yb))

    d_rows = sum(heights[2:])
    done = jnp.concatenate(solved, axis=2).transpose(1, 0, 2)
    done = lax.all_to_all(done, "row", 0, 0, tiled=True)
    done = done.reshape(rows_n, 2, sub, d_rows).transpose(3, 1, 0, 2).reshape(d_rows, cols)
    head_kept = jnp.concatenate([out0_kept, y_kept1], axis=0)
    head_sent = jnp.concatenate([out0_sent, y_sent1], axis=0)
    head = by_core(
        jnp.concatenate([head_kept, head_sent], axis=1), jnp.concatenate([head_sent, head_kept], axis=1)
    )
    return jnp.concatenate([head, done.astype(F32)], axis=0)[None, None]


def solution(mesh):
    in_specs = (
        P("leaf", "row", None, None),
        P("leaf", "row", None, None),
        P("leaf", "row", None, None),
        P("leaf", "row", None),
    )
    out_specs = P("leaf", "row", None, None)
    return jax.shard_map(shards, mesh=mesh, in_specs=in_specs, out_specs=out_specs, check_vma=False)
```

```python
import jax
import jax.numpy as jnp
import numpy as np
from jax import lax
from jax.experimental import pallas as pl
from jax.experimental.pallas import tpu as pltpu
from jax.sharding import PartitionSpec as P

F32 = jnp.float32
BF16 = jnp.bfloat16


def column_start(ancestor, source, width_all):
    offset = 0
    for higher in range(1, ancestor):
        for within in range(higher):
            offset += width_all // 2**within
    for within in range(source):
        offset += width_all // 2**within
    return offset


def dot(a, b):
    return jnp.dot(a, b, preferred_element_type=F32)


def dot_t(a, b):
    return lax.dot_general(a, b, (((1,), (b.ndim - 1,)), ((), ())), preferred_element_type=F32)


def core_swap(block):
    count = lax.axis_size("leaf")
    return lax.ppermute(block, "leaf", [(i, i ^ 1) for i in range(count)])


def leaf_groups(size):
    count = lax.axis_size("leaf")
    return [[first + i for i in range(size)] for first in range(0, count, size)]


def leaf_scatter(pieces):
    size = pieces.shape[0]
    return lax.all_to_all(pieces, "leaf", 0, 0, tiled=True, axis_index_groups=leaf_groups(size))


def leaf_everyone(block, size):
    return leaf_scatter(jnp.broadcast_to(block, (size, *block.shape)))


def pack_upper(off_diag, inv_diag, live, pairs, d_start):
    strip, width = off_diag.shape[2], inv_diag.shape[3]
    d_rows = inv_diag.shape[2] - d_start
    first = min(column_start(m, l, width) for m, l in pairs) // 128 * 128
    span = off_diag.shape[3] - first
    total = sum(width >> l for _, l in pairs)

    def body(live_ref, off_ref, inv_ref, out_ref, p_ref, d_ref, sems):
        p_copy = pltpu.make_async_copy(off_ref.at[0, 0, :, pl.ds(first, span)], p_ref, sems.at[0])
        d_copy = pltpu.make_async_copy(inv_ref.at[0, 0, pl.ds(d_start, d_rows), :], d_ref, sems.at[1])
        p_copy.start()
        d_copy.start()
        d_copy.wait()
        out_ref[strip:, :] = jnp.zeros((out_ref.shape[0] - strip, total), BF16)
        out_ref[strip : strip + d_rows, :width] = d_ref[...]
        p_copy.wait()
        at = 0
        for m, l in pairs:
            low = column_start(m, l, width) - first
            wide = width >> l
            alive = live_ref[m * (m - 1) // 2 + l].astype(F32)
            block = p_ref[:, low : low + wide].astype(F32) * alive
            out_ref[:strip, at : at + wide] = block.astype(BF16)
            at += wide

    tall = (strip + d_rows + 15) // 16 * 16
    return pl.pallas_call(
        body,
        out_shape=jax.ShapeDtypeStruct((tall, total), BF16),
        in_specs=[
            pl.BlockSpec(memory_space=pltpu.SMEM),
            pl.BlockSpec(memory_space=pl.ANY),
            pl.BlockSpec(memory_space=pl.ANY),
        ],
        out_specs=pl.BlockSpec(memory_space=pltpu.VMEM),
        scratch_shapes=[
            pltpu.VMEM((strip, span), BF16),
            pltpu.VMEM((d_rows, width), BF16),
            pltpu.SemaphoreType.DMA((2,)),
        ],
        compiler_params=pltpu.CompilerParams(vmem_limit_bytes=8 << 20),
        name="pack_upper",
    )(live, off_diag, inv_diag)


def level_zero(core, live, inverse, z_left, z_right, off_diag, placed):
    rows_n, both, width = inverse.shape
    half = z_left.shape[1]
    strip = off_diag.shape[2]
    under = both - strip
    parts = 2
    tall = width // parts
    each = rows_n // parts

    def body(core_ref, live_ref, inv_ref, left_ref, right_ref, off_ref, placed_ref, *rest):
        y_ref, kept_ref, sent_ref, d1_ref, d_ref, zl_ref, zr_ref, p_ref, sems = rest

        def d_copy(r):
            dst = d_ref.at[pl.ds(strip * r, strip), :]
            return pltpu.make_async_copy(inv_ref.at[r, pl.ds(0, strip), :], dst, sems.at[r])

        def d1_copy(r):
            dst = d1_ref.at[pl.ds(under * r, under), :]
            return pltpu.make_async_copy(inv_ref.at[r, pl.ds(strip, under), :], dst, sems.at[rows_n + r])

        left = pltpu.make_async_copy(left_ref, zl_ref, sems.at[2 * rows_n])
        right = pltpu.make_async_copy(right_ref, zr_ref, sems.at[2 * rows_n + 1])
        panel = pltpu.make_async_copy(off_ref.at[0, 0, :, pl.ds(0, width)], p_ref, sems.at[2 * rows_n + 2])
        left.start()
        right.start()
        for r in range(rows_n):
            d_copy(r).start()
        panel.start()
        for r in range(rows_n):
            d1_copy(r).start()
        left.wait()
        right.wait()
        first_core = core_ref[0] == 0
        z_kept = jnp.where(first_core, zl_ref[...], zr_ref[...])
        z_sent = jnp.where(first_core, zr_ref[...], zl_ref[...])
        z = jnp.concatenate([z_kept, z_sent], axis=1)
        total = jnp.zeros((strip, 2 * half), F32)
        for i in range(parts):
            for r in range(each * i, each * (i + 1)):
                d_copy(r).wait()
            y = dot(d_ref[tall * i : tall * (i + 1), :], z).astype(BF16)
            y_ref[tall * i : tall * (i + 1), :] = y
            if i == 0:
                panel.wait()
            total = total + dot(p_ref[:, tall * i : tall * (i + 1)], y)
        v = placed_ref[...] - total * live_ref[0].astype(F32)
        kept_ref[...] = v[:, :half]
        sent_ref[...] = v[:, half:].astype(BF16)
        for r in range(rows_n):
            d1_copy(r).wait()

    vmem = pl.BlockSpec(memory_space=pltpu.VMEM)
    smem = pl.BlockSpec(memory_space=pltpu.SMEM)
    hbm = pl.BlockSpec(memory_space=pltpu.HBM)
    anywhere = pl.BlockSpec(memory_space=pl.ANY)
    return pl.pallas_call(
        body,
        out_shape=(
            jax.ShapeDtypeStruct((width, 2 * half), BF16),
            jax.ShapeDtypeStruct((strip, half), F32),
            jax.ShapeDtypeStruct((strip, half), BF16),
            jax.ShapeDtypeStruct((rows_n * under, width), BF16),
        ),
        in_specs=[smem, smem, hbm, anywhere, anywhere, anywhere, vmem],
        out_specs=(vmem, vmem, vmem, anywhere),
        scratch_shapes=[
            pltpu.VMEM((width, width), BF16),
            pltpu.VMEM((width, half), BF16),
            pltpu.VMEM((width, half), BF16),
            pltpu.VMEM((strip, width), BF16),
            pltpu.SemaphoreType.DMA((2 * rows_n + 3,)),
        ],
        compiler_params=pltpu.CompilerParams(vmem_limit_bytes=20 << 20),
        name="level_zero",
    )(core, live, inverse, z_left, z_right, off_diag, placed)


def shards(rhs, inv_diag, off_diag, pair_mask):
    rows_n = lax.axis_size("row")
    leaves = lax.axis_size("leaf")
    levels = leaves.bit_length() - 1
    width = inv_diag.shape[3]
    cols = rhs.shape[3]
    strip = width // rows_n
    half = cols // 2
    sub = half // rows_n
    leaf = lax.axis_index("leaf")
    core = leaf & 1
    first_core = core == 0
    b_all = rhs[0, 0]
    d_all = inv_diag[0, 0]
    panels = off_diag[0, 0]
    live = pair_mask[0, 0]
    heights = [strip >> m for m in range(levels + 1)]
    starts = [sum(heights[:m]) for m in range(levels + 1)]

    def panel(m, l):
        first = column_start(m, l, width)
        return panels[:, first : first + (width >> l)]

    def mask_rows(l):
        ancestors = range(l + 1, levels + 1)
        index = jnp.asarray(np.repeat([m * (m - 1) // 2 + l for m in ancestors], strip), jnp.int32)
        hit = index[:, None] == lax.broadcasted_iota(jnp.int32, (1, live.shape[0]), 1)
        return jnp.where(hit, live[None], 0).sum(axis=1, keepdims=True).astype(F32)

    def by_core(one, two):
        return jnp.where(first_core, one, two)

    d_low = lax.all_gather(d_all[: starts[2]], "row", axis=0, tiled=False)
    b0 = b_all[: heights[0]]
    z0_left = lax.all_gather(b0[:, :half], "row", axis=0, tiled=True)
    z0_right = lax.all_gather(b0[:, half:], "row", axis=0, tiled=True)

    upper_pairs = sorted(
        ((m, l) for l in range(2, levels) for m in range(l + 1, levels + 1)), key=lambda p: (p[1], p[0])
    )
    d_first = {m: strip + starts[m] - starts[2] for m in range(2, levels + 1)}
    packed = pack_upper(off_diag, inv_diag, live, upper_pairs, starts[2])
    packed, z0_left = lax.optimization_barrier((packed, z0_left))
    everyone = lax.all_gather(packed, "row", axis=0, tiled=False)

    tall = strip * levels
    base = np.concatenate([strip * (m - 1) + np.arange(heights[m]) for m in range(1, levels + 1)])
    bits = np.concatenate([np.full(heights[m], 2**m - 1) for m in range(1, levels + 1)])
    step = np.concatenate([np.full(heights[m], heights[m]) for m in range(1, levels + 1)])
    place = jnp.asarray(base, jnp.int32) + (leaf & jnp.asarray(bits, jnp.int32)) * jnp.asarray(step, jnp.int32)
    spread = (lax.broadcasted_iota(jnp.int32, (tall, base.size), 0) == place[None]).astype(BF16)
    b_up = b_all[strip:]
    b_up = by_core(b_up, jnp.concatenate([b_up[:, half:], b_up[:, :half]], axis=1))
    placed = dot(spread, b_up)

    mask0, mask1 = lax.optimization_barrier((mask_rows(0), mask_rows(1)))
    yb0, kept, sent, d_leaf1 = level_zero(
        core.reshape(1), live, d_low, z0_left, z0_right, off_diag, placed[:strip]
    )
    got = core_swap(sent)
    parts = [
        placed[strip * (m - 1) : strip * m] - dot(panel(m, 0), yb0) * mask0[strip * (m - 1) : strip * m]
        for m in range(2, levels + 1)
    ]

    z1 = (kept + got.astype(F32)).astype(BF16)
    z1 = lax.all_gather(z1, "row", axis=0, tiled=False)
    z1 = z1.reshape(rows_n, 2, heights[1], half).transpose(1, 0, 2, 3).reshape(width, half)
    z1_got = core_swap(z1)
    yb_kept1 = dot(d_leaf1, z1).astype(BF16)
    z1_got, yb_kept1, parts = lax.optimization_barrier((z1_got, yb_kept1, parts))
    yb1 = jnp.concatenate([yb_kept1, dot(d_leaf1, z1_got).astype(BF16)], axis=1)
    yb1 = lax.optimization_barrier(yb1)
    d_own0 = d_all[: heights[0]]
    d_own1 = d_all[starts[1] : starts[2]]
    y_kept1 = dot(d_own1, z1)
    y_sent1 = dot(d_own1, z1_got)
    out0_kept = dot(d_own0, by_core(z0_left, z0_right))
    out0_sent = dot(d_own0, by_core(z0_right, z0_left))
    part = jnp.concatenate(
        [
            parts[m - 2] - dot(panel(m, 1), yb1) * mask1[strip * (m - 2) : strip * (m - 1)]
            for m in range(2, levels + 1)
        ],
        axis=0,
    )
    part = part[:, :half] + core_swap(part[:, half:].astype(BF16)).astype(F32)
    p_rows = strip * (levels - 1)

    turned = part.T.astype(BF16).reshape(rows_n, sub, p_rows)
    turned = lax.all_to_all(turned, "row", 0, 0, tiled=True)

    def turned_of(m):
        return turned[:, :, (m - 2) * strip : (m - 1) * strip]

    def d_leaf(m):
        rows = everyone[:, d_first[m] : d_first[m] + heights[m], :width]
        return rows.reshape(rows_n * heights[m], width)

    p_leaf = {}
    at = 0
    for m, l in upper_pairs:
        p_leaf[m, l] = everyone[:, :strip, at : at + (width >> l)]
        at += width >> l

    def natural(z, m):
        z = z.reshape(rows_n, 2 * sub, 2**m, heights[m])
        return z.transpose(1, 2, 0, 3).reshape(2 * sub, width)

    solved = []
    terms = {m: [] for m in range(3, levels + 1)}
    for m in range(2, levels + 1):
        if m == 2:
            pieces = leaf_everyone(turned_of(2), 4).astype(F32)
            pieces = pieces.reshape(2, 2, rows_n, sub, strip).sum(axis=0).astype(BF16)
            z = pieces.transpose(1, 0, 2, 3).reshape(rows_n, 2 * sub, strip)
        else:
            size = 2**m
            mine = jnp.where(
                (jnp.arange(2) == core)[None, :, None, None], turned_of(m)[:, None], jnp.zeros((), BF16)
            ).reshape(rows_n, 2 * sub, strip)
            v = mine.astype(F32)
            for l, yb in terms[m]:
                v = v - dot_t(yb, p_leaf[m, l]).transpose(1, 0, 2)
            v = v.astype(BF16).reshape(size, rows_n * 2 * sub // size, strip)
            z = leaf_scatter(v).astype(F32).sum(axis=0).astype(BF16)
            z = leaf_everyone(z, size).reshape(rows_n, 2 * sub, strip)
        y = dot_t(natural(z, m), d_leaf(m))
        yb = y.astype(BF16)
        solved.append(yb.reshape(2 * sub, rows_n, heights[m]))
        for higher in range(m + 1, levels + 1):
            terms[higher].append((m, yb))

    d_rows = sum(heights[2:])
    done = jnp.concatenate(solved, axis=2).transpose(1, 0, 2)
    done = lax.all_to_all(done, "row", 0, 0, tiled=True)
    done = done.reshape(rows_n, 2, sub, d_rows).transpose(3, 1, 0, 2).reshape(d_rows, cols)
    head_kept = jnp.concatenate([out0_kept, y_kept1], axis=0)
    head_sent = jnp.concatenate([out0_sent, y_sent1], axis=0)
    head = by_core(
        jnp.concatenate([head_kept, head_sent], axis=1), jnp.concatenate([head_sent, head_kept], axis=1)
    )
    return jnp.concatenate([head, done.astype(F32)], axis=0)[None, None]


def solution(mesh):
    in_specs = (
        P("leaf", "row", None, None),
        P("leaf", "row", None, None),
        P("leaf", "row", None, None),
        P("leaf", "row", None),
    )
    out_specs = P("leaf", "row", None, None)
    return jax.shard_map(shards, mesh=mesh, in_specs=in_specs, out_specs=out_specs, check_vma=False)
```

```python
import jax
import jax.numpy as jnp
import numpy as np
from jax import lax
from jax.experimental import pallas as pl
from jax.experimental.pallas import tpu as pltpu
from jax.sharding import PartitionSpec as P

F32 = jnp.float32
BF16 = jnp.bfloat16


def column_start(ancestor, source, width_all):
    offset = 0
    for higher in range(1, ancestor):
        for within in range(higher):
            offset += width_all // 2**within
    for within in range(source):
        offset += width_all // 2**within
    return offset


def dot(a, b):
    return jnp.dot(a, b, preferred_element_type=F32)


def dot_t(a, b):
    return lax.dot_general(a, b, (((1,), (b.ndim - 1,)), ((), ())), preferred_element_type=F32)


def core_swap(block):
    count = lax.axis_size("leaf")
    return lax.ppermute(block, "leaf", [(i, i ^ 1) for i in range(count)])


def leaf_groups(size):
    count = lax.axis_size("leaf")
    return [[first + i for i in range(size)] for first in range(0, count, size)]


def leaf_scatter(pieces):
    size = pieces.shape[0]
    return lax.all_to_all(pieces, "leaf", 0, 0, tiled=True, axis_index_groups=leaf_groups(size))


def leaf_everyone(block, size):
    return leaf_scatter(jnp.broadcast_to(block, (size, *block.shape)))


def pack_upper(off_diag, inv_diag, live, pairs, d_start):
    strip, width = off_diag.shape[2], inv_diag.shape[3]
    d_rows = inv_diag.shape[2] - d_start
    first = min(column_start(m, l, width) for m, l in pairs) // 128 * 128
    span = off_diag.shape[3] - first
    total = sum(width >> l for _, l in pairs)

    def body(live_ref, off_ref, inv_ref, out_ref, p_ref, d_ref, sems):
        p_copy = pltpu.make_async_copy(off_ref.at[0, 0, :, pl.ds(first, span)], p_ref, sems.at[0])
        d_copy = pltpu.make_async_copy(inv_ref.at[0, 0, pl.ds(d_start, d_rows), :], d_ref, sems.at[1])
        p_copy.start()
        d_copy.start()
        d_copy.wait()
        out_ref[strip:, :] = jnp.zeros((out_ref.shape[0] - strip, total), BF16)
        out_ref[strip : strip + d_rows, :width] = d_ref[...]
        p_copy.wait()
        at = 0
        for m, l in pairs:
            low = column_start(m, l, width) - first
            wide = width >> l
            alive = live_ref[m * (m - 1) // 2 + l].astype(F32)
            block = p_ref[:, low : low + wide].astype(F32) * alive
            out_ref[:strip, at : at + wide] = block.astype(BF16)
            at += wide

    tall = (strip + d_rows + 15) // 16 * 16
    return pl.pallas_call(
        body,
        out_shape=jax.ShapeDtypeStruct((tall, total), BF16),
        in_specs=[
            pl.BlockSpec(memory_space=pltpu.SMEM),
            pl.BlockSpec(memory_space=pl.ANY),
            pl.BlockSpec(memory_space=pl.ANY),
        ],
        out_specs=pl.BlockSpec(memory_space=pltpu.VMEM),
        scratch_shapes=[
            pltpu.VMEM((strip, span), BF16),
            pltpu.VMEM((d_rows, width), BF16),
            pltpu.SemaphoreType.DMA((2,)),
        ],
        name="pack_upper",
    )(live, off_diag, inv_diag)


def shards(rhs, inv_diag, off_diag, pair_mask):
    rows_n = lax.axis_size("row")
    leaves = lax.axis_size("leaf")
    levels = leaves.bit_length() - 1
    width = inv_diag.shape[3]
    cols = rhs.shape[3]
    strip = width // rows_n
    half = cols // 2
    sub = half // rows_n
    leaf = lax.axis_index("leaf")
    core = leaf & 1
    first_core = core == 0
    b_all = rhs[0, 0]
    d_all = inv_diag[0, 0]
    panels = off_diag[0, 0]
    live = pair_mask[0, 0]
    heights = [strip >> m for m in range(levels + 1)]
    starts = [sum(heights[:m]) for m in range(levels + 1)]

    def panel(m, l):
        first = column_start(m, l, width)
        return panels[:, first : first + (width >> l)]

    def mask_rows(l):
        ancestors = range(l + 1, levels + 1)
        index = jnp.asarray(np.repeat([m * (m - 1) // 2 + l for m in ancestors], strip), jnp.int32)
        hit = index[:, None] == lax.broadcasted_iota(jnp.int32, (1, live.shape[0]), 1)
        return jnp.where(hit, live[None], 0).sum(axis=1, keepdims=True).astype(F32)

    def by_core(one, two):
        return jnp.where(first_core, one, two)

    d_low = lax.all_gather(d_all[: starts[2]], "row", axis=0, tiled=False)
    b0 = b_all[: heights[0]]
    z0_left = lax.all_gather(b0[:, :half], "row", axis=0, tiled=True)
    z0_right = lax.all_gather(b0[:, half:], "row", axis=0, tiled=True)

    upper_pairs = sorted(
        ((m, l) for l in range(2, levels) for m in range(l + 1, levels + 1)), key=lambda p: (p[1], p[0])
    )
    d_first = {m: strip + starts[m] - starts[2] for m in range(2, levels + 1)}
    packed = pack_upper(off_diag, inv_diag, live, upper_pairs, starts[2])
    packed, z0_left = lax.optimization_barrier((packed, z0_left))
    everyone = lax.all_gather(packed, "row", axis=0, tiled=False)

    tall = strip * levels
    base = np.concatenate([strip * (m - 1) + np.arange(heights[m]) for m in range(1, levels + 1)])
    bits = np.concatenate([np.full(heights[m], 2**m - 1) for m in range(1, levels + 1)])
    step = np.concatenate([np.full(heights[m], heights[m]) for m in range(1, levels + 1)])
    place = jnp.asarray(base, jnp.int32) + (leaf & jnp.asarray(bits, jnp.int32)) * jnp.asarray(step, jnp.int32)
    spread = (lax.broadcasted_iota(jnp.int32, (tall, base.size), 0) == place[None]).astype(BF16)
    b_up = b_all[strip:]
    b_up = by_core(b_up, jnp.concatenate([b_up[:, half:], b_up[:, :half]], axis=1))
    placed = dot(spread, b_up)

    z0_sent = by_core(z0_right, z0_left)
    z0_kept = by_core(z0_left, z0_right)
    mask0, mask1 = lax.optimization_barrier((mask_rows(0), mask_rows(1)))
    live1 = mask0[:strip]
    d_full0 = d_low[:, :strip].reshape(width, width)
    d_leaf1 = d_low[:, strip:].reshape(rows_n * heights[1], width)
    yb_sent = dot(d_full0, z0_sent).astype(BF16)
    sent = placed[:strip, half:] - dot(panel(1, 0), yb_sent) * live1
    got = core_swap(sent.astype(BF16))
    yb_kept = dot(d_full0, z0_kept).astype(BF16)
    kept = placed[:strip, :half] - dot(panel(1, 0), yb_kept) * live1
    yb0 = jnp.concatenate([yb_kept, yb_sent], axis=1)
    parts = [
        placed[strip * (m - 1) : strip * m] - dot(panel(m, 0), yb0) * mask0[strip * (m - 1) : strip * m]
        for m in range(2, levels + 1)
    ]

    z1 = (kept + got.astype(F32)).astype(BF16)
    z1 = lax.all_gather(z1, "row", axis=0, tiled=False)
    z1 = z1.reshape(rows_n, 2, heights[1], half).transpose(1, 0, 2, 3).reshape(width, half)
    z1_got = core_swap(z1)
    yb_kept1 = dot(d_leaf1, z1).astype(BF16)
    z1_got, yb_kept1, parts = lax.optimization_barrier((z1_got, yb_kept1, parts))
    yb1 = jnp.concatenate([yb_kept1, dot(d_leaf1, z1_got).astype(BF16)], axis=1)
    yb1 = lax.optimization_barrier(yb1)
    d_own0 = d_all[: heights[0]]
    d_own1 = d_all[starts[1] : starts[2]]
    y_kept1 = dot(d_own1, z1)
    y_sent1 = dot(d_own1, z1_got)
    out0_kept = dot(d_own0, z0_kept)
    out0_sent = dot(d_own0, z0_sent)
    part = jnp.concatenate(
        [
            parts[m - 2] - dot(panel(m, 1), yb1) * mask1[strip * (m - 2) : strip * (m - 1)]
            for m in range(2, levels + 1)
        ],
        axis=0,
    )
    part = part[:, :half] + core_swap(part[:, half:].astype(BF16)).astype(F32)
    p_rows = strip * (levels - 1)

    turned = part.T.astype(BF16).reshape(rows_n, sub, p_rows)
    turned = lax.all_to_all(turned, "row", 0, 0, tiled=True)

    def turned_of(m):
        return turned[:, :, (m - 2) * strip : (m - 1) * strip]

    def d_leaf(m):
        rows = everyone[:, d_first[m] : d_first[m] + heights[m], :width]
        return rows.reshape(rows_n * heights[m], width)

    p_leaf = {}
    at = 0
    for m, l in upper_pairs:
        p_leaf[m, l] = everyone[:, :strip, at : at + (width >> l)]
        at += width >> l

    def natural(z, m):
        z = z.reshape(rows_n, 2 * sub, 2**m, heights[m])
        return z.transpose(1, 2, 0, 3).reshape(2 * sub, width)

    solved = []
    sums = {}
    for m in range(2, levels + 1):
        if m == 2:
            pieces = leaf_everyone(turned_of(2), 4).astype(F32)
            pieces = pieces.reshape(2, 2, rows_n, sub, strip).sum(axis=0).astype(BF16)
            z = pieces.transpose(1, 0, 2, 3).reshape(rows_n, 2 * sub, strip)
        else:
            size = 2**m
            mine = jnp.where(
                (jnp.arange(2) == core)[None, :, None, None], turned_of(m)[:, None], jnp.zeros((), BF16)
            ).reshape(rows_n, 2 * sub, strip)
            v = (mine.astype(F32) - sums[m]).astype(BF16)
            v = v.reshape(size, rows_n * 2 * sub // size, strip)
            z = leaf_scatter(v).astype(F32).sum(axis=0).astype(BF16)
            z = leaf_everyone(z, size).reshape(rows_n, 2 * sub, strip)
        y = dot_t(natural(z, m), d_leaf(m))
        yb = y.astype(BF16)
        solved.append(yb.reshape(2 * sub, rows_n, heights[m]))
        for higher in range(m + 1, levels + 1):
            term = dot_t(yb, p_leaf[higher, m]).transpose(1, 0, 2)
            sums[higher] = term if m == 2 else sums[higher] + term

    d_rows = sum(heights[2:])
    done = jnp.concatenate(solved, axis=2).transpose(1, 0, 2)
    done = lax.all_to_all(done, "row", 0, 0, tiled=True)
    done = done.reshape(rows_n, 2, sub, d_rows).transpose(3, 1, 0, 2).reshape(d_rows, cols)
    head_kept = jnp.concatenate([out0_kept, y_kept1], axis=0)
    head_sent = jnp.concatenate([out0_sent, y_sent1], axis=0)
    head = by_core(
        jnp.concatenate([head_kept, head_sent], axis=1), jnp.concatenate([head_sent, head_kept], axis=1)
    )
    return jnp.concatenate([head, done.astype(F32)], axis=0)[None, None]


def solution(mesh):
    in_specs = (
        P("leaf", "row", None, None),
        P("leaf", "row", None, None),
        P("leaf", "row", None, None),
        P("leaf", "row", None),
    )
    out_specs = P("leaf", "row", None, None)
    return jax.shard_map(shards, mesh=mesh, in_specs=in_specs, out_specs=out_specs, check_vma=False)
```

```python
import jax
import jax.numpy as jnp
import numpy as np
from jax import lax
from jax.experimental import pallas as pl
from jax.experimental.pallas import tpu as pltpu
from jax.sharding import PartitionSpec as P

F32 = jnp.float32
BF16 = jnp.bfloat16


def column_start(ancestor, source, width_all):
    offset = 0
    for higher in range(1, ancestor):
        for within in range(higher):
            offset += width_all // 2**within
    for within in range(source):
        offset += width_all // 2**within
    return offset


def dot(a, b):
    return jnp.dot(a, b, preferred_element_type=F32)


def dot_t(a, b):
    return lax.dot_general(a, b, (((1,), (b.ndim - 1,)), ((), ())), preferred_element_type=F32)


def core_swap(block):
    count = lax.axis_size("leaf")
    return lax.ppermute(block, "leaf", [(i, i ^ 1) for i in range(count)])


def leaf_groups(size):
    count = lax.axis_size("leaf")
    return [[first + i for i in range(size)] for first in range(0, count, size)]


def leaf_scatter(pieces):
    size = pieces.shape[0]
    return lax.all_to_all(pieces, "leaf", 0, 0, tiled=True, axis_index_groups=leaf_groups(size))


def leaf_everyone(block, size):
    return leaf_scatter(jnp.broadcast_to(block, (size, *block.shape)))


def pack_upper(off_diag, inv_diag, live, pairs, d_start):
    strip, width = off_diag.shape[2], inv_diag.shape[3]
    d_rows = inv_diag.shape[2] - d_start
    first = min(column_start(m, l, width) for m, l in pairs) // 128 * 128
    span = off_diag.shape[3] - first
    total = sum(width >> l for _, l in pairs)

    def body(live_ref, off_ref, inv_ref, out_ref, p_ref, d_ref, sems):
        p_copy = pltpu.make_async_copy(off_ref.at[0, 0, :, pl.ds(first, span)], p_ref, sems.at[0])
        d_copy = pltpu.make_async_copy(inv_ref.at[0, 0, pl.ds(d_start, d_rows), :], d_ref, sems.at[1])
        p_copy.start()
        d_copy.start()
        d_copy.wait()
        out_ref[strip:, :] = jnp.zeros((out_ref.shape[0] - strip, total), BF16)
        out_ref[strip : strip + d_rows, :width] = d_ref[...]
        p_copy.wait()
        at = 0
        for m, l in pairs:
            low = column_start(m, l, width) - first
            wide = width >> l
            alive = live_ref[m * (m - 1) // 2 + l].astype(F32)
            block = p_ref[:, low : low + wide].astype(F32) * alive
            out_ref[:strip, at : at + wide] = block.astype(BF16)
            at += wide

    tall = (strip + d_rows + 15) // 16 * 16
    return pl.pallas_call(
        body,
        out_shape=jax.ShapeDtypeStruct((tall, total), BF16),
        in_specs=[
            pl.BlockSpec(memory_space=pltpu.SMEM),
            pl.BlockSpec(memory_space=pl.ANY),
            pl.BlockSpec(memory_space=pl.ANY),
        ],
        out_specs=pl.BlockSpec(memory_space=pltpu.VMEM),
        scratch_shapes=[
            pltpu.VMEM((strip, span), BF16),
            pltpu.VMEM((d_rows, width), BF16),
            pltpu.SemaphoreType.DMA((2,)),
        ],
        name="pack_upper",
    )(live, off_diag, inv_diag)


def shards(rhs, inv_diag, off_diag, pair_mask):
    rows_n = lax.axis_size("row")
    leaves = lax.axis_size("leaf")
    levels = leaves.bit_length() - 1
    width = inv_diag.shape[3]
    cols = rhs.shape[3]
    strip = width // rows_n
    half = cols // 2
    sub = half // rows_n
    leaf = lax.axis_index("leaf")
    core = leaf & 1
    first_core = core == 0
    b_all = rhs[0, 0]
    d_all = inv_diag[0, 0]
    panels = off_diag[0, 0]
    live = pair_mask[0, 0]
    heights = [strip >> m for m in range(levels + 1)]
    starts = [sum(heights[:m]) for m in range(levels + 1)]

    def panel(m, l):
        first = column_start(m, l, width)
        return panels[:, first : first + (width >> l)]

    def mask_rows(l):
        ancestors = range(l + 1, levels + 1)
        index = jnp.asarray(np.repeat([m * (m - 1) // 2 + l for m in ancestors], strip), jnp.int32)
        hit = index[:, None] == lax.broadcasted_iota(jnp.int32, (1, live.shape[0]), 1)
        return jnp.where(hit, live[None], 0).sum(axis=1, keepdims=True).astype(F32)

    def by_core(one, two):
        return jnp.where(first_core, one, two)

    d_own0 = d_all[: heights[0]]
    d_full0 = lax.all_gather(d_own0, "row", axis=0, tiled=True)
    b0 = b_all[: heights[0]]
    z0_left = lax.all_gather(b0[:, :half], "row", axis=0, tiled=True)
    z0_right = lax.all_gather(b0[:, half:], "row", axis=0, tiled=True)

    upper_pairs = sorted(
        ((m, l) for l in range(2, levels) for m in range(l + 1, levels + 1)), key=lambda p: (p[1], p[0])
    )
    d_first = {m: strip + starts[m] - starts[2] for m in range(2, levels + 1)}
    packed = pack_upper(off_diag, inv_diag, live, upper_pairs, starts[2])
    packed, z0_left = lax.optimization_barrier((packed, z0_left))
    everyone = lax.all_gather(packed, "row", axis=0, tiled=False)

    tall = strip * levels
    base = np.concatenate([strip * (m - 1) + np.arange(heights[m]) for m in range(1, levels + 1)])
    bits = np.concatenate([np.full(heights[m], 2**m - 1) for m in range(1, levels + 1)])
    step = np.concatenate([np.full(heights[m], heights[m]) for m in range(1, levels + 1)])
    place = jnp.asarray(base, jnp.int32) + (leaf & jnp.asarray(bits, jnp.int32)) * jnp.asarray(step, jnp.int32)
    spread = (lax.broadcasted_iota(jnp.int32, (tall, base.size), 0) == place[None]).astype(BF16)
    b_up = b_all[strip:]
    b_up = by_core(b_up, jnp.concatenate([b_up[:, half:], b_up[:, :half]], axis=1))
    placed = dot(spread, b_up)

    z0 = jnp.concatenate([by_core(z0_left, z0_right), by_core(z0_right, z0_left)], axis=1)
    mask0, mask1 = lax.optimization_barrier((mask_rows(0), mask_rows(1)))
    yb0 = dot(d_full0, z0).astype(BF16)
    part1 = placed[:strip] - dot(panel(1, 0), yb0) * mask0[:strip]
    kept = part1[:, :half]
    got = core_swap(part1[:, half:].astype(BF16))
    parts = [
        placed[strip * (m - 1) : strip * m] - dot(panel(m, 0), yb0) * mask0[strip * (m - 1) : strip * m]
        for m in range(2, levels + 1)
    ]

    d_own1 = d_all[starts[1] : starts[2]]
    z1 = (kept + got.astype(F32)).astype(BF16)
    z1 = lax.all_gather(z1, "row", axis=0, tiled=False)
    z1 = z1.reshape(rows_n, 2, heights[1], half).transpose(1, 0, 2, 3).reshape(width, half)
    z1_got = core_swap(z1)
    y_kept1 = dot(d_own1, z1)
    y_sent1 = dot(d_own1, z1_got)
    yb1 = jnp.concatenate([y_kept1, y_sent1], axis=1).astype(BF16)
    yb1, parts = lax.optimization_barrier((yb1, parts))
    yb1 = lax.all_gather(yb1, "row", axis=0, tiled=True)
    out0 = dot(d_own0, z0)
    part = jnp.concatenate(
        [
            parts[m - 2] - dot(panel(m, 1), yb1) * mask1[strip * (m - 2) : strip * (m - 1)]
            for m in range(2, levels + 1)
        ],
        axis=0,
    )
    part = part[:, :half] + core_swap(part[:, half:].astype(BF16)).astype(F32)
    p_rows = strip * (levels - 1)

    turned = part.T.astype(BF16).reshape(rows_n, sub, p_rows)
    turned = lax.all_to_all(turned, "row", 0, 0, tiled=True)

    def turned_of(m):
        return turned[:, :, (m - 2) * strip : (m - 1) * strip]

    p_first = {}
    at = 0
    for m, l in upper_pairs:
        p_first[m, l] = at
        at += width >> l

    def d_leaf(m, block):
        rows = block[:, d_first[m] : d_first[m] + heights[m], :width]
        return rows.reshape(rows_n * heights[m], width)

    def p_leaf(m, l, block):
        return block[:, :strip, p_first[m, l] : p_first[m, l] + (width >> l)]

    def natural(z, m):
        z = z.reshape(rows_n, 2 * sub, 2**m, heights[m])
        return z.transpose(1, 2, 0, 3).reshape(2 * sub, width)

    solved = []
    sums = {}
    for m in range(2, levels + 1):
        if m == 2:
            pieces = jnp.broadcast_to(turned_of(2), (4, rows_n, sub, strip))
            pieces, everyone = lax.optimization_barrier((pieces, everyone))
            pieces = leaf_scatter(pieces).astype(F32)
            pieces = pieces.reshape(2, 2, rows_n, sub, strip).sum(axis=0).astype(BF16)
            z = pieces.transpose(1, 0, 2, 3).reshape(rows_n, 2 * sub, strip)
        else:
            size = 2**m
            mine = jnp.where(
                (jnp.arange(2) == core)[None, :, None, None], turned_of(m)[:, None], jnp.zeros((), BF16)
            ).reshape(rows_n, 2 * sub, strip)
            v = (mine.astype(F32) - sums[m]).astype(BF16)
            v = v.reshape(size, rows_n * 2 * sub // size, strip)
            z = leaf_scatter(v).astype(F32).sum(axis=0).astype(BF16)
            z = leaf_everyone(z, size).reshape(rows_n, 2 * sub, strip)
        y = dot_t(natural(z, m), d_leaf(m, everyone))
        yb = y.astype(BF16)
        solved.append(yb.reshape(2 * sub, rows_n, heights[m]))
        for higher in range(m + 1, levels + 1):
            term = dot_t(yb, p_leaf(higher, m, everyone)).transpose(1, 0, 2)
            sums[higher] = term if m == 2 else sums[higher] + term

    d_rows = sum(heights[2:])
    done = jnp.concatenate(solved, axis=2).transpose(1, 0, 2)
    done = lax.all_to_all(done, "row", 0, 0, tiled=True)
    done = done.reshape(rows_n, 2, sub, d_rows).transpose(3, 1, 0, 2).reshape(d_rows, cols)
    head_kept = jnp.concatenate([out0[:, :half], y_kept1], axis=0)
    head_sent = jnp.concatenate([out0[:, half:], y_sent1], axis=0)
    head = by_core(
        jnp.concatenate([head_kept, head_sent], axis=1), jnp.concatenate([head_sent, head_kept], axis=1)
    )
    return jnp.concatenate([head, done.astype(F32)], axis=0)[None, None]


def solution(mesh):
    in_specs = (
        P("leaf", "row", None, None),
        P("leaf", "row", None, None),
        P("leaf", "row", None, None),
        P("leaf", "row", None),
    )
    out_specs = P("leaf", "row", None, None)
    return jax.shard_map(shards, mesh=mesh, in_specs=in_specs, out_specs=out_specs, check_vma=False)
```

```python
import jax
import jax.numpy as jnp
import numpy as np
from jax import lax
from jax.experimental import pallas as pl
from jax.experimental.pallas import tpu as pltpu
from jax.sharding import PartitionSpec as P

F32 = jnp.float32
BF16 = jnp.bfloat16


def column_start(ancestor, source, width_all):
    offset = 0
    for higher in range(1, ancestor):
        for within in range(higher):
            offset += width_all // 2**within
    for within in range(source):
        offset += width_all // 2**within
    return offset


def dot(a, b):
    return jnp.dot(a, b, preferred_element_type=F32)


def dot_t(a, b):
    return lax.dot_general(a, b, (((1,), (b.ndim - 1,)), ((), ())), preferred_element_type=F32)


def core_swap(block):
    count = lax.axis_size("leaf")
    return lax.ppermute(block, "leaf", [(i, i ^ 1) for i in range(count)])


def leaf_groups(size):
    count = lax.axis_size("leaf")
    return [[first + i for i in range(size)] for first in range(0, count, size)]


def leaf_scatter(pieces):
    size = pieces.shape[0]
    return lax.all_to_all(pieces, "leaf", 0, 0, tiled=True, axis_index_groups=leaf_groups(size))


def leaf_everyone(block, size):
    return leaf_scatter(jnp.broadcast_to(block, (size, *block.shape)))


def pack_upper(off_diag, inv_diag, live, pairs, d_start):
    strip, width = off_diag.shape[2], inv_diag.shape[3]
    d_rows = inv_diag.shape[2] - d_start
    first = min(column_start(m, l, width) for m, l in pairs) // 128 * 128
    span = off_diag.shape[3] - first
    total = sum(width >> l for _, l in pairs)

    def body(live_ref, off_ref, inv_ref, out_ref, p_ref, d_ref, sems):
        p_copy = pltpu.make_async_copy(off_ref.at[0, 0, :, pl.ds(first, span)], p_ref, sems.at[0])
        d_copy = pltpu.make_async_copy(inv_ref.at[0, 0, pl.ds(d_start, d_rows), :], d_ref, sems.at[1])
        p_copy.start()
        d_copy.start()
        d_copy.wait()
        out_ref[strip:, :] = jnp.zeros((out_ref.shape[0] - strip, total), BF16)
        out_ref[strip : strip + d_rows, :width] = d_ref[...]
        p_copy.wait()
        at = 0
        for m, l in pairs:
            low = column_start(m, l, width) - first
            wide = width >> l
            alive = live_ref[m * (m - 1) // 2 + l].astype(F32)
            block = p_ref[:, low : low + wide].astype(F32) * alive
            out_ref[:strip, at : at + wide] = block.astype(BF16)
            at += wide

    tall = (strip + d_rows + 15) // 16 * 16
    return pl.pallas_call(
        body,
        out_shape=jax.ShapeDtypeStruct((tall, total), BF16),
        in_specs=[
            pl.BlockSpec(memory_space=pltpu.SMEM),
            pl.BlockSpec(memory_space=pl.ANY),
            pl.BlockSpec(memory_space=pl.ANY),
        ],
        out_specs=pl.BlockSpec(memory_space=pltpu.VMEM),
        scratch_shapes=[
            pltpu.VMEM((strip, span), BF16),
            pltpu.VMEM((d_rows, width), BF16),
            pltpu.SemaphoreType.DMA((2,)),
        ],
        name="pack_upper",
    )(live, off_diag, inv_diag)


def shards(rhs, inv_diag, off_diag, pair_mask):
    rows_n = lax.axis_size("row")
    leaves = lax.axis_size("leaf")
    levels = leaves.bit_length() - 1
    width = inv_diag.shape[3]
    cols = rhs.shape[3]
    strip = width // rows_n
    half = cols // 2
    sub = half // rows_n
    leaf = lax.axis_index("leaf")
    core = leaf & 1
    first_core = core == 0
    b_all = rhs[0, 0]
    d_all = inv_diag[0, 0]
    panels = off_diag[0, 0]
    live = pair_mask[0, 0]
    heights = [strip >> m for m in range(levels + 1)]
    starts = [sum(heights[:m]) for m in range(levels + 1)]

    def panel(m, l):
        first = column_start(m, l, width)
        return panels[:, first : first + (width >> l)]

    def mask_rows(l):
        ancestors = range(l + 1, levels + 1)
        index = jnp.asarray(np.repeat([m * (m - 1) // 2 + l for m in ancestors], strip), jnp.int32)
        hit = index[:, None] == lax.broadcasted_iota(jnp.int32, (1, live.shape[0]), 1)
        return jnp.where(hit, live[None], 0).sum(axis=1, keepdims=True).astype(F32)

    def by_core(one, two):
        return jnp.where(first_core, one, two)

    d_own0 = d_all[: heights[0]]
    d_full0 = lax.all_gather(d_own0, "row", axis=0, tiled=True)
    b0 = b_all[: heights[0]]
    z0_left = lax.all_gather(b0[:, :half], "row", axis=0, tiled=True)
    z0_right = lax.all_gather(b0[:, half:], "row", axis=0, tiled=True)

    upper_pairs = sorted(
        ((m, l) for l in range(2, levels) for m in range(l + 1, levels + 1)), key=lambda p: (p[1], p[0])
    )
    d_first = {m: strip + starts[m] - starts[2] for m in range(2, levels + 1)}
    packed = pack_upper(off_diag, inv_diag, live, upper_pairs, starts[2])
    packed, z0_left = lax.optimization_barrier((packed, z0_left))
    everyone = lax.all_gather(packed, "row", axis=0, tiled=False)

    tall = strip * levels
    base = np.concatenate([strip * (m - 1) + np.arange(heights[m]) for m in range(1, levels + 1)])
    bits = np.concatenate([np.full(heights[m], 2**m - 1) for m in range(1, levels + 1)])
    step = np.concatenate([np.full(heights[m], heights[m]) for m in range(1, levels + 1)])
    place = jnp.asarray(base, jnp.int32) + (leaf & jnp.asarray(bits, jnp.int32)) * jnp.asarray(step, jnp.int32)
    spread = (lax.broadcasted_iota(jnp.int32, (tall, base.size), 0) == place[None]).astype(BF16)
    b_up = b_all[strip:]
    b_up = by_core(b_up, jnp.concatenate([b_up[:, half:], b_up[:, :half]], axis=1))
    placed = dot(spread, b_up)

    z0 = jnp.concatenate([by_core(z0_left, z0_right), by_core(z0_right, z0_left)], axis=1)
    mask0, mask1 = lax.optimization_barrier((mask_rows(0), mask_rows(1)))
    yb0 = dot(d_full0, z0).astype(BF16)
    part1 = placed[:strip] - dot(panel(1, 0), yb0) * mask0[:strip]
    kept = part1[:, :half]
    got = core_swap(part1[:, half:].astype(BF16))
    parts = [
        placed[strip * (m - 1) : strip * m] - dot(panel(m, 0), yb0) * mask0[strip * (m - 1) : strip * m]
        for m in range(2, levels + 1)
    ]

    d_own1 = d_all[starts[1] : starts[2]]
    z1 = (kept + got.astype(F32)).astype(BF16)
    z1 = lax.all_gather(z1, "row", axis=0, tiled=False)
    z1 = z1.reshape(rows_n, 2, heights[1], half).transpose(1, 0, 2, 3).reshape(width, half)
    z1_got = core_swap(z1)
    y_kept1 = dot(d_own1, z1)
    y_sent1 = dot(d_own1, z1_got)
    yb1 = jnp.concatenate([y_kept1, y_sent1], axis=1).astype(BF16)
    yb1, parts = lax.optimization_barrier((yb1, parts))
    yb1 = lax.all_gather(yb1, "row", axis=0, tiled=True)
    out0 = dot(d_own0, z0)
    part = jnp.concatenate(
        [
            parts[m - 2] - dot(panel(m, 1), yb1) * mask1[strip * (m - 2) : strip * (m - 1)]
            for m in range(2, levels + 1)
        ],
        axis=0,
    )
    part = part[:, :half] + core_swap(part[:, half:].astype(BF16)).astype(F32)
    p_rows = strip * (levels - 1)

    turned = part.T.astype(BF16).reshape(rows_n, sub, p_rows)
    turned = lax.all_to_all(turned, "row", 0, 0, tiled=True)

    def turned_of(m):
        return turned[:, :, (m - 2) * strip : (m - 1) * strip]

    p_first = {}
    at = 0
    for m, l in upper_pairs:
        p_first[m, l] = at
        at += width >> l

    def d_leaf(m, block):
        rows = block[:, d_first[m] : d_first[m] + heights[m], :width]
        return rows.reshape(rows_n * heights[m], width)

    def p_leaf(m, l, block):
        return block[:, :strip, p_first[m, l] : p_first[m, l] + (width >> l)]

    def natural(z, m):
        z = z.reshape(rows_n, 2 * sub, 2**m, heights[m])
        return z.transpose(1, 2, 0, 3).reshape(2 * sub, width)

    solved = []
    sums = {}
    for m in range(2, levels + 1):
        if m == 2:
            pieces = jnp.broadcast_to(turned_of(2), (4, rows_n, sub, strip))
            pieces, everyone = lax.optimization_barrier((pieces, everyone))
            pieces = leaf_scatter(pieces).astype(F32)
            pieces = pieces.reshape(2, 2, rows_n, sub, strip).sum(axis=0).astype(BF16)
            z = pieces.transpose(1, 0, 2, 3).reshape(rows_n, 2 * sub, strip)
        else:
            size = 2**m
            mine = jnp.where(
                (jnp.arange(2) == core)[None, :, None, None], turned_of(m)[:, None], jnp.zeros((), BF16)
            ).reshape(rows_n, 2 * sub, strip)
            v = (mine.astype(F32) - sums[m]).astype(BF16)
            v = v.reshape(size, rows_n * 2 * sub // size, strip)
            z = leaf_scatter(v).astype(F32).sum(axis=0).astype(BF16)
            z = leaf_everyone(z, size).reshape(rows_n, 2 * sub, strip)
        y = dot_t(natural(z, m), d_leaf(m, everyone))
        yb = y.astype(BF16)
        solved.append(yb.reshape(2 * sub, rows_n, heights[m]))
        for higher in range(m + 1, levels + 1):
            block = p_leaf(higher, m, everyone)
            if higher == m + 1:
                block = lax.optimization_barrier(block)
            term = dot_t(yb, block).transpose(1, 0, 2)
            sums[higher] = term if m == 2 else sums[higher] + term

    d_rows = sum(heights[2:])
    done = jnp.concatenate(solved, axis=2).transpose(1, 0, 2)
    done = lax.all_to_all(done, "row", 0, 0, tiled=True)
    done = done.reshape(rows_n, 2, sub, d_rows).transpose(3, 1, 0, 2).reshape(d_rows, cols)
    head_kept = jnp.concatenate([out0[:, :half], y_kept1], axis=0)
    head_sent = jnp.concatenate([out0[:, half:], y_sent1], axis=0)
    head = by_core(
        jnp.concatenate([head_kept, head_sent], axis=1), jnp.concatenate([head_sent, head_kept], axis=1)
    )
    return jnp.concatenate([head, done.astype(F32)], axis=0)[None, None]


def solution(mesh):
    in_specs = (
        P("leaf", "row", None, None),
        P("leaf", "row", None, None),
        P("leaf", "row", None, None),
        P("leaf", "row", None),
    )
    out_specs = P("leaf", "row", None, None)
    return jax.shard_map(shards, mesh=mesh, in_specs=in_specs, out_specs=out_specs, check_vma=False)
```

```python
import jax
import jax.numpy as jnp
import numpy as np
from jax import lax
from jax.experimental import pallas as pl
from jax.experimental.pallas import tpu as pltpu
from jax.sharding import PartitionSpec as P

F32 = jnp.float32
BF16 = jnp.bfloat16


def column_start(ancestor, source, width_all):
    offset = 0
    for higher in range(1, ancestor):
        for within in range(higher):
            offset += width_all // 2**within
    for within in range(source):
        offset += width_all // 2**within
    return offset


def dot(a, b):
    return jnp.dot(a, b, preferred_element_type=F32)


def dot_t(a, b):
    return lax.dot_general(a, b, (((1,), (b.ndim - 1,)), ((), ())), preferred_element_type=F32)


def core_swap(block):
    count = lax.axis_size("leaf")
    return lax.ppermute(block, "leaf", [(i, i ^ 1) for i in range(count)])


def leaf_groups(size):
    count = lax.axis_size("leaf")
    return [[first + i for i in range(size)] for first in range(0, count, size)]


def leaf_scatter(pieces):
    size = pieces.shape[0]
    return lax.all_to_all(pieces, "leaf", 0, 0, tiled=True, axis_index_groups=leaf_groups(size))


def leaf_everyone(block, size):
    return leaf_scatter(jnp.broadcast_to(block, (size, *block.shape)))


def pack_upper(off_diag, inverse, live, pairs):
    strip = off_diag.shape[2]
    d_rows, width = inverse.shape
    first = min(column_start(m, l, width) for m, l in pairs) // 128 * 128
    span = off_diag.shape[3] - first
    total = sum(width >> l for _, l in pairs)

    def body(live_ref, off_ref, inv_ref, out_ref, p_ref, sems):
        p_copy = pltpu.make_async_copy(off_ref.at[0, 0, :, pl.ds(first, span)], p_ref, sems.at[0])
        p_copy.start()
        out_ref[strip:, :] = jnp.zeros((out_ref.shape[0] - strip, total), BF16)
        out_ref[strip : strip + d_rows, :width] = inv_ref[...]
        p_copy.wait()
        at = 0
        for m, l in pairs:
            low = column_start(m, l, width) - first
            wide = width >> l
            alive = live_ref[m * (m - 1) // 2 + l].astype(F32)
            block = p_ref[:, low : low + wide].astype(F32) * alive
            out_ref[:strip, at : at + wide] = block.astype(BF16)
            at += wide

    tall = (strip + d_rows + 15) // 16 * 16
    return pl.pallas_call(
        body,
        out_shape=jax.ShapeDtypeStruct((tall, total), BF16),
        in_specs=[
            pl.BlockSpec(memory_space=pltpu.SMEM),
            pl.BlockSpec(memory_space=pl.ANY),
            pl.BlockSpec(memory_space=pltpu.VMEM),
        ],
        out_specs=pl.BlockSpec(memory_space=pltpu.VMEM),
        scratch_shapes=[
            pltpu.VMEM((strip, span), BF16),
            pltpu.SemaphoreType.DMA((1,)),
        ],
        name="pack_upper",
    )(live, off_diag, inverse)


def shards(rhs, inv_diag, off_diag, pair_mask):
    rows_n = lax.axis_size("row")
    leaves = lax.axis_size("leaf")
    levels = leaves.bit_length() - 1
    width = inv_diag.shape[3]
    cols = rhs.shape[3]
    strip = width // rows_n
    half = cols // 2
    sub = half // rows_n
    leaf = lax.axis_index("leaf")
    core = leaf & 1
    first_core = core == 0
    b_all = rhs[0, 0]
    d_all = inv_diag[0, 0]
    panels = off_diag[0, 0]
    live = pair_mask[0, 0]
    heights = [strip >> m for m in range(levels + 1)]
    starts = [sum(heights[:m]) for m in range(levels + 1)]

    def panel(m, l):
        first = column_start(m, l, width)
        return panels[:, first : first + (width >> l)]

    def mask_rows(l):
        ancestors = range(l + 1, levels + 1)
        index = jnp.asarray(np.repeat([m * (m - 1) // 2 + l for m in ancestors], strip), jnp.int32)
        hit = index[:, None] == lax.broadcasted_iota(jnp.int32, (1, live.shape[0]), 1)
        return jnp.where(hit, live[None], 0).sum(axis=1, keepdims=True).astype(F32)

    def by_core(one, two):
        return jnp.where(first_core, one, two)

    d_own0 = d_all[: heights[0]]
    d_full0 = lax.all_gather(d_own0, "row", axis=0, tiled=True)
    b0 = b_all[: heights[0]]
    z0_left = lax.all_gather(b0[:, :half], "row", axis=0, tiled=True)
    z0_right = lax.all_gather(b0[:, half:], "row", axis=0, tiled=True)

    upper_pairs = sorted(
        ((m, l) for l in range(2, levels) for m in range(l + 1, levels + 1)), key=lambda p: (p[1], p[0])
    )
    d_first = {m: strip + starts[m] - starts[2] for m in range(2, levels + 1)}
    turned_levels = (2, levels)
    tail, live_up, z0_right = lax.optimization_barrier((d_all[starts[2] :], live, z0_right))

    def in_order(m):
        rows = tail[starts[m] - starts[2] : starts[m] - starts[2] + heights[m]]
        if m not in turned_levels:
            return rows
        rows = rows.reshape(heights[m], 2**m, rows_n, heights[m])
        return rows.transpose(0, 2, 1, 3).reshape(heights[m], width)

    inverse_up = jnp.concatenate([in_order(m) for m in range(2, levels + 1)], axis=0)
    packed = pack_upper(off_diag, inverse_up, live_up, upper_pairs)
    packed, z0_right = lax.optimization_barrier((packed, z0_right))
    everyone = lax.all_gather(packed, "row", axis=0, tiled=False)

    tall = strip * levels
    base = np.concatenate([strip * (m - 1) + np.arange(heights[m]) for m in range(1, levels + 1)])
    bits = np.concatenate([np.full(heights[m], 2**m - 1) for m in range(1, levels + 1)])
    step = np.concatenate([np.full(heights[m], heights[m]) for m in range(1, levels + 1)])
    place = jnp.asarray(base, jnp.int32) + (leaf & jnp.asarray(bits, jnp.int32)) * jnp.asarray(step, jnp.int32)
    spread = (lax.broadcasted_iota(jnp.int32, (tall, base.size), 0) == place[None]).astype(BF16)
    b_up = b_all[strip:]
    b_up = by_core(b_up, jnp.concatenate([b_up[:, half:], b_up[:, :half]], axis=1))
    placed = dot(spread, b_up)

    z0 = jnp.concatenate([by_core(z0_left, z0_right), by_core(z0_right, z0_left)], axis=1)
    mask0, mask1 = lax.optimization_barrier((mask_rows(0), mask_rows(1)))
    yb0 = dot(d_full0, z0).astype(BF16)
    part1 = placed[:strip] - dot(panel(1, 0), yb0) * mask0[:strip]
    kept = part1[:, :half]
    got = core_swap(part1[:, half:].astype(BF16))
    parts = [
        placed[strip * (m - 1) : strip * m] - dot(panel(m, 0), yb0) * mask0[strip * (m - 1) : strip * m]
        for m in range(2, levels + 1)
    ]

    d_own1 = d_all[starts[1] : starts[2]]
    z1 = (kept + got.astype(F32)).astype(BF16)
    z1 = lax.all_gather(z1, "row", axis=0, tiled=False)
    z1 = z1.reshape(rows_n, 2, heights[1], half).transpose(1, 0, 2, 3).reshape(width, half)
    z1_got = core_swap(z1)
    y_kept1 = dot(d_own1, z1)
    y_sent1 = dot(d_own1, z1_got)
    yb1 = jnp.concatenate([y_kept1, y_sent1], axis=1).astype(BF16)
    yb1, parts = lax.optimization_barrier((yb1, parts))
    yb1 = lax.all_gather(yb1, "row", axis=0, tiled=True)
    out0 = dot(d_own0, z0)
    part = jnp.concatenate(
        [
            parts[m - 2] - dot(panel(m, 1), yb1) * mask1[strip * (m - 2) : strip * (m - 1)]
            for m in range(2, levels + 1)
        ],
        axis=0,
    )
    part = part[:, :half] + core_swap(part[:, half:].astype(BF16)).astype(F32)
    p_rows = strip * (levels - 1)

    turned = part.T.astype(BF16).reshape(rows_n, sub, p_rows)
    turned = lax.all_to_all(turned, "row", 0, 0, tiled=True)

    def turned_of(m):
        return turned[:, :, (m - 2) * strip : (m - 1) * strip]

    p_first = {}
    at = 0
    for m, l in upper_pairs:
        p_first[m, l] = at
        at += width >> l

    def d_leaf(m, block):
        rows = block[:, d_first[m] : d_first[m] + heights[m], :width]
        return rows.reshape(rows_n * heights[m], width)

    def p_leaf(m, l, block):
        return block[:, :strip, p_first[m, l] : p_first[m, l] + (width >> l)]

    def natural(z, m):
        if m in turned_levels:
            return z.transpose(1, 0, 2).reshape(2 * sub, width)
        z = z.reshape(rows_n, 2 * sub, 2**m, heights[m])
        return z.transpose(1, 2, 0, 3).reshape(2 * sub, width)

    solved = []
    sums = {}
    for m in range(2, levels + 1):
        if m == 2:
            pieces = jnp.broadcast_to(turned_of(2), (4, rows_n, sub, strip))
            pieces, everyone = lax.optimization_barrier((pieces, everyone))
            pieces = leaf_scatter(pieces).astype(F32)
            pieces = pieces.reshape(2, 2, rows_n, sub, strip).sum(axis=0).astype(BF16)
            z = pieces.transpose(1, 0, 2, 3).reshape(rows_n, 2 * sub, strip)
        else:
            size = 2**m
            mine = jnp.where(
                (jnp.arange(2) == core)[None, :, None, None], turned_of(m)[:, None], jnp.zeros((), BF16)
            ).reshape(rows_n, 2 * sub, strip)
            v = (mine.astype(F32) - sums[m]).astype(BF16)
            v = v.reshape(size, rows_n * 2 * sub // size, strip)
            z = leaf_scatter(v).astype(F32).sum(axis=0).astype(BF16)
            z = leaf_everyone(z, size).reshape(rows_n, 2 * sub, strip)
        y = dot_t(natural(z, m), d_leaf(m, everyone))
        yb = y.astype(BF16)
        solved.append(yb.reshape(2 * sub, rows_n, heights[m]))
        for higher in range(m + 1, levels + 1):
            term = dot_t(yb, p_leaf(higher, m, everyone)).transpose(1, 0, 2)
            sums[higher] = term if m == 2 else sums[higher] + term

    d_rows = sum(heights[2:])
    done = jnp.concatenate(solved, axis=2).transpose(1, 0, 2)
    done = lax.all_to_all(done, "row", 0, 0, tiled=True)
    done = done.reshape(rows_n, 2, sub, d_rows).transpose(3, 1, 0, 2).reshape(d_rows, cols)
    head_kept = jnp.concatenate([out0[:, :half], y_kept1], axis=0)
    head_sent = jnp.concatenate([out0[:, half:], y_sent1], axis=0)
    head = by_core(
        jnp.concatenate([head_kept, head_sent], axis=1), jnp.concatenate([head_sent, head_kept], axis=1)
    )
    return jnp.concatenate([head, done.astype(F32)], axis=0)[None, None]


def solution(mesh):
    in_specs = (
        P("leaf", "row", None, None),
        P("leaf", "row", None, None),
        P("leaf", "row", None, None),
        P("leaf", "row", None),
    )
    out_specs = P("leaf", "row", None, None)
    return jax.shard_map(shards, mesh=mesh, in_specs=in_specs, out_specs=out_specs, check_vma=False)
```
